32 devices in a mesh: freq: 8 (over y, x, core), recv: 4 (over z).
Axes of the slice: x: 2, y: 2, z: 4, core: 2. Of those that a mesh axis runs over, the one named last changes fastest.
Arguments:
- response: bfloat16 [2, 256, 128, 4096], P(None, 'freq', 'recv'), may hold values from -0.0625 to 0.0625
- focusing: float32 [2, 256, 16, 4096], P(None, 'freq', None, 'recv'), may hold values from -6 to 6
- window_onset: int32 [16, 128], P(None, ('recv', 'freq')), may hold values from 0 to 511
- window_end: int32 [16, 128], P(None, ('recv', 'freq')), may hold values from 128 to 1023, as said below
Outputs:
- windowed: float32 [16, 128, 1024], P(None, ('recv', 'freq'))
The draws below stay inside these ranges and needn't reach their ends.
Inputs may be any that keep to these rules, and one draw needn't show every extreme that they name: window_end - window_onset lies between 128 and 512 for every trace.
All inputs are finite; a program needn't handle non-finite values.
Results may differ from the reference program's by a relative error of at most 0.0029.
Values may be sent and summed in bfloat16 or wider, within the bound.
A program may use at most 64 MiB of HBM per device.

```python
import math
import jax
import jax.numpy as jnp
from jax import lax

NF = 256
NT = 1024
NS = 4096
F = 16
NR = 128


def window_pair(key):
    onset = jax.random.randint(jax.random.fold_in(key, 11), (F, NR), 0, NT // 2)
    length = jax.random.randint(jax.random.fold_in(key, 12), (F, NR), NT // 8, NT // 2 + 1)
    return (onset.astype(jnp.int32), (onset + length).astype(jnp.int32))


def draw_window_onset(key, part):
    return window_pair(key)[0]


def draw_window_end(key, part):
    return window_pair(key)[1]


def level_of(stream_key, dims, split, low, top_value):
    loudness, own = 1.0, jax.random.fold_in(stream_key, 6)
    for axis_at, blocks in split:
        draws = jnp.exp(jax.random.uniform(jax.random.fold_in(own, axis_at), (blocks,), jnp.float32, low / len(split), top_value / len(split)))
        loudness = loudness * jnp.repeat(draws, dims[axis_at] // blocks).reshape([-1 if axis == axis_at else 1 for axis in range(len(dims))])
    return loudness


def normal_values(stream_key, shape, spread, bound, pieces=(), kind=jnp.bfloat16):
    factor_of = level_of(stream_key, shape, pieces, -0.22, 0.18) if pieces else 1.0
    array = jax.random.normal(stream_key, shape, jnp.float32) * spread * factor_of
    return jnp.minimum(jnp.maximum(array, -bound), bound).astype(kind)


def setup_inputs(seed: int = 0) -> dict:
    keys = jax.random.split(jax.random.key(seed), 5)
    response = normal_values(keys[0], (2, NF, NR, NS), (2 * NS) ** -0.5, 0.0625, ((1, 8), (2, 4)))
    focusing = normal_values(keys[1], (2, NF, F, NS), 1.0, 6.0, ((1, 8), (3, 4)), jnp.float32)
    window_onset = draw_window_onset(jax.random.fold_in(keys[4], 71), 0)
    window_end = draw_window_end(jax.random.fold_in(keys[4], 71), 0)
    return {"response": response, "focusing": focusing, "window_onset": window_onset, "window_end": window_end}


def make_table(base, count):
    freqs = base + jnp.arange(count, dtype=jnp.int32)
    samples = jnp.arange(NT, dtype=jnp.int32)
    phase = (freqs[:, None] * samples[None, :] % NT).astype(jnp.float32) * (2.0 * math.pi / NT)
    scale = 1.0 / math.sqrt(NF)
    return jnp.stack([jnp.cos(phase) * scale, -jnp.sin(phase) * scale])

def reference(response, focusing, window_onset, window_end):
    focus_half = focusing.astype(jnp.bfloat16)

    def one_freq(index):
        real_resp = response[0, index]
        imag_resp = response[1, index]
        real_focus = focus_half[0, index]
        imag_focus = focus_half[1, index]
        real_part = jnp.dot(real_resp, real_focus.T, preferred_element_type=jnp.float32) - jnp.dot(imag_resp, imag_focus.T, preferred_element_type=jnp.float32)
        imag_part = jnp.dot(real_resp, imag_focus.T, preferred_element_type=jnp.float32) + jnp.dot(imag_resp, real_focus.T, preferred_element_type=jnp.float32)
        return jnp.stack([real_part, imag_part])
    spectra = lax.map(one_freq, jnp.arange(NF, dtype=jnp.int32))
    table = make_table(0, NF)
    traces = jnp.einsum('kcrq,ckt->qrt', spectra, table, precision=lax.Precision.HIGHEST)
    samples = jnp.arange(NT, dtype=jnp.int32)
    keep = (samples[None, None, :] >= window_onset[:, :, None]) & (samples[None, None, :] < window_end[:, :, None])
    return jnp.where(keep, traces, jnp.float32(0.0))
```

```python
import functools
import math

import jax
import jax.numpy as jnp
import numpy as np
from jax import lax
from jax.experimental import pallas as pl
from jax.experimental.pallas import tpu as pltpu
from jax.sharding import PartitionSpec as P

NT = 1024
LANES = 128
MESH = pl.DeviceIdType.MESH


def make_tables(across, groups, per):
    freqs = groups * per
    count = across * freqs
    phase = (np.arange(count)[:, None] * np.arange(NT)[None, :] % NT) * (2.0 * math.pi / NT)
    scale = 1.0 / math.sqrt(count)
    table = np.stack([np.cos(phase) * scale, -np.sin(phase) * scale], 1)
    table = table.reshape(across, groups, per, 2, NT).transpose(1, 2, 3, 0, 4).reshape(-1, NT)
    high = table.astype(np.float32).astype(jnp.bfloat16)
    low = (table - high.astype(np.float64)).astype(np.float32).astype(jnp.bfloat16)
    return np.stack([high, low])


def lent_freqs(line, freqs, rows, focal):
    if line < 4:
        return 0
    return min(freqs, (line - 2) * freqs * focal // (focal + rows))


def spectra_kernel(
    line, across, lent, extra, batch, resp_hbm, focus_hbm, table_hbm, onset_hbm, end_hbm, out_ref,
    resp, focus, held, guest, acc, back, back_out, back_in, last_out, last_in, table, onset, finale, traces,
    early_out, early_in, early_rows, late_out, late_in, late_rows, back_rows,
    resp_sem, focus_sem, table_sem, onset_sem, finale_sem, send_sem, recv_sem, fine_send, fine_recv,
    guest_send, guest_recv, back_send, back_recv, x_send, x_recv, x_local,
):
    me = lax.axis_index("recv")
    mine = lax.axis_index("freq")
    _, freqs, rows, _ = resp_hbm.shape
    focal, depth = focus_hbm.shape[2], focus_hbm.shape[3]
    groups = acc.shape[0]
    per = freqs // groups
    owned = rows // across
    kept = groups - lent
    whole = kept - 1 if extra else kept
    rest = per - extra
    has_left, has_right = me > 0, me < line - 1
    is_first, is_last = me == 0, me == line - 1
    left, right = jnp.maximum(me - 1, 0), jnp.minimum(me + 1, line - 1)

    def load_focus(g):
        return pltpu.make_async_copy(
            focus_hbm.at[:, pl.ds(g * per, per)], focus.at[:, pl.ds(g * per, per)], focus_sem.at[g]
        )

    def load_resp(g):
        return pltpu.make_async_copy(
            resp_hbm.at[:, pl.ds(g * per, per)], resp.at[:, pl.ds(g * per, per)], resp_sem.at[g]
        )

    barrier = pltpu.get_barrier_semaphore()

    @pl.when(has_left)
    def _():
        pl.semaphore_signal(barrier, inc=1, device_id={"recv": left}, device_id_type=MESH)

    @pl.when(has_right)
    def _():
        pl.semaphore_signal(barrier, inc=1, device_id={"recv": right}, device_id_type=MESH)

    for hop in range(1, across):
        other = lax.rem(mine + hop, across)
        pl.semaphore_signal(barrier, inc=1, device_id={"freq": other}, device_id_type=MESH)

    for g in range(groups):
        load_focus(g).start()
    for g in range(groups):
        load_resp(g).start()

    load_table = pltpu.make_async_copy(table_hbm, table, table_sem)
    load_table.start()
    load_onset = pltpu.make_async_copy(onset_hbm, onset, onset_sem)
    load_onset.start()
    load_finale = pltpu.make_async_copy(end_hbm, finale, finale_sem)
    load_finale.start()

    def convert(g):
        load_focus(g).wait()
        for i in range(per):
            k = g * per + i
            for part in range(2):
                held[me, k, part * focal:(part + 1) * focal, :] = focus[part, k].astype(jnp.bfloat16)

    for g in range(min(2, groups)):
        convert(g)

    beside = has_left.astype(jnp.int32) + has_right.astype(jnp.int32)
    pl.semaphore_wait(barrier, across - 1 + beside)

    def hand_on(way, step, block, g, target):
        piece = held.at[block, pl.ds(g * per, per)]
        return pltpu.make_async_remote_copy(
            src_ref=piece, dst_ref=piece,
            send_sem=send_sem.at[way, step, g], recv_sem=recv_sem.at[block, g],
            device_id={"recv": target}, device_id_type=MESH,
        )

    def hand_part(way, block, target):
        piece = held.at[block, pl.ds(whole * per, rest)]
        return pltpu.make_async_remote_copy(
            src_ref=piece, dst_ref=piece,
            send_sem=send_sem.at[way, 0, whole], recv_sem=recv_sem.at[block, whole],
            device_id={"recv": target}, device_id_type=MESH,
        )

    def own_right(g):
        return has_right & ((me < line - 2) | (g < whole)) if lent + extra else has_right

    def own_left(g):
        return has_left & ((me > 1) | (g < whole)) if lent + extra else has_left

    def lend(i, target):
        columns = pl.ds(pl.multiple_of(target * depth, LANES), depth)
        return pltpu.make_async_remote_copy(
            src_ref=resp.at[:, pl.ds((kept + i) * per, per), :, columns], dst_ref=guest.at[i],
            send_sem=guest_send.at[i], recv_sem=guest_recv.at[i],
            device_id={"recv": target}, device_id_type=MESH,
        )

    def lend_last(n, target):
        columns = pl.ds(pl.multiple_of(target * depth, LANES), depth)
        return pltpu.make_async_remote_copy(
            src_ref=resp.at[:, pl.ds((groups - 1) * per + n, 1), :, columns],
            dst_ref=guest.at[lent - 1, :, pl.ds(n, 1)],
            send_sem=guest_send.at[lent + 1 + n], recv_sem=guest_recv.at[lent + 1 + n],
            device_id={"recv": target}, device_id_type=MESH,
        )

    def lend_part(target):
        columns = pl.ds(pl.multiple_of(target * depth, LANES), depth)
        return pltpu.make_async_remote_copy(
            src_ref=resp.at[:, pl.ds(whole * per + rest, extra), :, columns],
            dst_ref=guest.at[lent, :, pl.ds(0, extra)],
            send_sem=guest_send.at[lent], recv_sem=guest_recv.at[lent],
            device_id={"recv": target}, device_id_type=MESH,
        )

    def give_back(part, source, target, place):
        copies = []
        for other in range(across):
            copies.append(pltpu.make_async_remote_copy(
                src_ref=source.at[other], dst_ref=target.at[mine],
                send_sem=back_send.at[part, other], recv_sem=back_recv.at[part, mine],
                device_id={"recv": place, "freq": other}, device_id_type=MESH,
            ))
        return copies

    def take_back(part, source, target, place):
        copies = []
        for other in range(across):
            copies.append(pltpu.make_async_remote_copy(
                src_ref=source.at[other], dst_ref=target.at[other],
                send_sem=back_send.at[part, other], recv_sem=back_recv.at[part, other],
                device_id={"recv": place, "freq": other}, device_id_type=MESH,
            ))
        return copies

    def hand_last(way, block, n, target):
        piece = held.at[block, pl.ds((groups - 1) * per + n, 1)]
        return pltpu.make_async_remote_copy(
            src_ref=piece, dst_ref=piece,
            send_sem=fine_send.at[way, n], recv_sem=fine_recv.at[way, n],
            device_id={"recv": target}, device_id_type=MESH,
        )

    @pl.loop(0, groups)
    def _(g):
        @pl.when(own_right(g))
        def _():
            hand_on(0, 0, me, g, right).start()

        @pl.when(own_left(g))
        def _():
            hand_on(1, 0, me, g, left).start()

        @pl.when(g + 2 < groups)
        def _():
            convert(g + 2)

    if extra:
        @pl.when(me == line - 2)
        def _():
            hand_part(0, me, right).start()

        @pl.when(me == 1)
        def _():
            hand_part(1, me, left).start()

    def multiply(lhs, rhs):
        return lax.dot_general(
            lhs.reshape(2 * rows, depth), rhs, (((1,), (1,)), ((), ())),
            preferred_element_type=jnp.float32,
        )

    def products(left_of, block, g, first=0, last=per):
        parts = []
        for i in range(per):
            if not first <= i < last:
                parts.append(jnp.zeros((2 * rows, 2 * focal), jnp.float32))
                continue
            parts.append(multiply(left_of(i), held[block, g * per + i]))
        return jnp.concatenate(parts, axis=1)

    def of_block(block, g, last=per):
        columns = pl.ds(pl.multiple_of(block * depth, LANES), depth)
        return products(lambda i: resp[:, g * per + i, :, columns], block, g, 0, last)

    @pl.loop(0, groups)
    def _(g):
        load_resp(g).wait()

    if extra:
        @pl.when(is_first)
        def _():
            lend_part(right).start()

        @pl.when(is_last)
        def _():
            lend_part(left).start()

    for at_end, beside in ((is_first, right), (is_last, left)):
        @pl.when(at_end)
        def _():
            for i in range(lent - 1):
                lend(i, beside).start()
            for n in range(per if lent else 0):
                lend_last(n, beside).start()

    @pl.loop(0, groups)
    def _(g):
        acc[g] = of_block(me, g)

    half = lax.rem(lax.broadcasted_iota(jnp.int32, (rows, LANES), 1), 2 * focal) < focal

    def combine(tile):
        real, imag = tile[:rows], tile[rows:]
        return real + jnp.where(
            half, -pltpu.roll(imag, LANES - focal, axis=1), pltpu.roll(imag, focal, axis=1)
        )

    is_host = ((me == 1) | (me == line - 2)) if lent + extra else False
    end = jnp.where(me == 1, 0, line - 1)
    beside_end = jnp.where(is_first, right, left)
    fine = line > 2

    def serve(i):
        lend(i, end).wait_recv()
        back[i] = combine(products(lambda n: guest[i, :, n], me, kept + i))

    def forward(way, step, block, g, target):
        if not fine:
            hand_on(way, step, block, g, target).start()
            return
        last = (step == line - 2) & (g == groups - 1)

        @pl.when(last)
        def _():
            for n in range(per):
                hand_last(way, block, n, target).start()

        @pl.when(jnp.logical_not(last))
        def _():
            hand_on(way, step, block, g, target).start()

    def visit(t):
        step, g = 1 + t // groups, t % groups
        from_left, from_right = me - step, me + step
        due_left, due_right = from_left >= 0, from_right < line
        if lent + extra:
            due_left = due_left & ((step > 1) | (me < line - 1) | (g < whole))
            due_right = due_right & ((step > 1) | (me > 0) | (g < whole))
        left_block, right_block = jnp.maximum(from_left, 0), jnp.minimum(from_right, line - 1)

        @pl.when(due_left)
        def _():
            hand_on(0, 0, left_block, g, left).wait_recv()

            @pl.when(has_right & (step < line - 1))
            def _():
                forward(0, step, left_block, g, right)

        @pl.when(due_right)
        def _():
            hand_on(1, 0, right_block, g, right).wait_recv()

            @pl.when(has_left & (step < line - 1))
            def _():
                forward(1, step, right_block, g, left)

        @pl.loop(0, 2)
        def _(side):
            @pl.when(((side == 0) & due_left) | ((side == 1) & due_right))
            def _():
                acc[g] = acc[g] + of_block(jnp.where(side == 0, left_block, right_block), g)

        if extra:
            @pl.when((is_first | is_last) & (step == 1) & (g == groups - 1))
            def _():
                block = jnp.where(is_first, 1, line - 2)
                hand_part(jnp.where(is_first, 1, 0), block, beside_end).wait_recv()
                acc[whole] = acc[whole] + of_block(block, whole, rest)

            @pl.when(is_host & (step == line - 2) & (g == 0))
            def _():
                lend_part(end).wait_recv()
                tile = products(lambda n: guest[lent, :, n - rest], me, whole, rest)
                back[lent] = combine(tile)

        if batch:
            @pl.when(is_host & (step == line - 2))
            def _():
                turn = (g + 1) // 2
                first = jnp.where(g == groups - 1, turn - 1, jnp.where(g % 2 == 0, turn - 1, turn))
                until = jnp.where(g == groups - 1, lent - 1, turn)

                @pl.loop(jnp.maximum(jnp.minimum(first, lent - 1), 0), jnp.minimum(until, lent - 1))
                def _(i):
                    serve(i)

                @pl.when(g == groups - 1)
                def _():
                    for j, (slot, _group) in enumerate(batch):
                        for d in range(across):
                            back_out[d, j * owned:(j + 1) * owned, :] = back[
                                slot, d * owned:(d + 1) * owned, :
                            ]
                    for copy in give_back(0, back_out, back_in, end):
                        copy.start()

    def visit_end():
        @pl.when(is_first | is_last)
        def _():
            block = jnp.where(is_first, line - 1, 0)
            columns = pl.ds(pl.multiple_of(block * depth, LANES), depth)
            parts = []
            for n in range(per):
                hand_last(jnp.where(is_first, 1, 0), block, n, beside_end).wait_recv()
                k = (groups - 1) * per + n
                parts.append(multiply(resp[:, k, :, columns], held[block, k]))
            acc[groups - 1] = acc[groups - 1] + jnp.concatenate(parts, axis=1)

    @pl.loop(0, (line - 1) * groups - 1)
    def _(t):
        visit(t)

    def exchange(part, source, target):
        copies = []
        for hop in range(1, across):
            other = lax.rem(mine + hop, across)
            copies.append(pltpu.make_async_remote_copy(
                src_ref=source.at[other], dst_ref=target.at[mine],
                send_sem=x_send.at[part, hop], recv_sem=x_recv.at[part, hop],
                device_id={"freq": other}, device_id_type=MESH,
            ))
        copies.append(pltpu.make_async_copy(source.at[mine], target.at[mine], x_local.at[part]))
        return copies

    def arrange(source, target):
        count = target.shape[1]
        for f in range(across):
            for r in range(owned):
                lines = source[f, pl.ds(r, count, stride=owned), :] if count > 1 else source[f, r:r + 1, :]
                for g in range(count):
                    target[r, g, f:f + 1, :] = lines[g:g + 1]

    def transform(source, group):
        parts = []
        for g in range(source.shape[1]):
            for m in range(2 * per):
                lanes = [source[r, g, :, m * focal:(m + 1) * focal] for r in range(owned)]
                parts.append(jnp.concatenate(lanes, axis=1))
        values = jnp.concatenate(parts, axis=0)
        high = values.astype(jnp.bfloat16)
        low = (values - high.astype(jnp.float32)).astype(jnp.bfloat16)
        first = group * 2 * per * across
        span = slice(first, first + values.shape[0])

        def dot(a, b):
            return lax.dot_general(a, b, (((0,), (0,)), ((), ())), preferred_element_type=jnp.float32)

        return dot(high, table[0, span]) + (dot(low, table[0, span]) + dot(high, table[1, span]))

    for g in range(groups - 1):
        tile = combine(acc[g])
        for d in range(across):
            early_out[d, g * owned:(g + 1) * owned, :] = tile[d * owned:(d + 1) * owned]
    early = exchange(0, early_out, early_in)
    for copy in early:
        copy.start()
    load_table.wait()
    load_onset.wait()
    load_finale.wait()
    for copy in early:
        copy.wait()
    arrange(early_in, early_rows)
    traces[...] = transform(early_rows, 0)

    if fine:
        visit_end()
    else:
        visit((line - 1) * groups - 1)

    tile = combine(acc[groups - 1])
    for d in range(across):
        late_out[d] = tile[d * owned:(d + 1) * owned]
    late = exchange(1, late_out, late_in)
    for copy in late:
        copy.start()

    if lent:
        @pl.when(is_host)
        def _():
            parts = []
            for n in range(per):
                lend_last(n, end).wait_recv()
                parts.append(multiply(guest[lent - 1, :, n], held[me, (groups - 1) * per + n]))
            tile = combine(jnp.concatenate(parts, axis=1))
            for d in range(across):
                last_out[d] = tile[d * owned:(d + 1) * owned]
            for copy in give_back(1, last_out, last_in, end):
                copy.start()

    @pl.loop(0, (line - 1) * groups - (1 if fine else 0))
    def _(t):
        step, g = t // groups, t % groups

        @pl.when(has_right & (me - step >= 0) & ((step > 0) | own_right(g)))
        def _():
            hand_on(0, step, me, g, right).wait_send()

        @pl.when(has_left & (me + step < line) & ((step > 0) | own_left(g)))
        def _():
            hand_on(1, step, me, g, left).wait_send()

    if fine:
        for sender, way, beside in ((me == line - 2, 0, right), (me == 1, 1, left)):
            @pl.when(sender)
            def _():
                for n in range(per):
                    hand_last(way, me, n, beside).wait_send()

    if extra:
        @pl.when(me == line - 2)
        def _():
            hand_part(0, me, right).wait_send()

        @pl.when(me == 1)
        def _():
            hand_part(1, me, left).wait_send()

        @pl.when(is_first | is_last)
        def _():
            lend_part(me).wait_send()

    if lent:
        @pl.when(is_first | is_last)
        def _():
            for i in range(lent - 1):
                lend(i, me).wait_send()
            for n in range(per):
                lend_last(n, me).wait_send()

        @pl.when(is_host)
        def _():
            if batch:
                for copy in give_back(0, back_out, back_in, end):
                    copy.wait_send()
            for copy in give_back(1, last_out, last_in, end):
                copy.wait_send()

    samples = lax.broadcasted_iota(jnp.int32, (focal, NT), 1)
    starts, ends = jnp.transpose(onset[...]), jnp.transpose(finale[...])
    if batch:
        @pl.when(is_first | is_last)
        def _():
            for copy in take_back(0, back_out, back_in, beside_end):
                copy.wait_recv()
            arrange(back_in, back_rows)
            traces[...] = traces[...] + transform(back_rows, batch[0][1])

    for copy in late:
        copy.wait()
    arrange(late_in, late_rows)
    if lent:
        @pl.when(is_first | is_last)
        def _():
            for copy in take_back(1, last_out, last_in, beside_end):
                copy.wait_recv()
            for f in range(across):
                for r in range(owned):
                    late_rows[r, 0, f:f + 1, :] = late_rows[r, 0, f:f + 1, :] + last_in[f, r:r + 1, :]
    total = traces[...] + transform(late_rows, groups - 1)
    for r in range(owned):
        inside = (samples >= starts[:, r:r + 1]) & (samples < ends[:, r:r + 1])
        windowed = jnp.where(inside, total[r * focal:(r + 1) * focal], 0.0)
        for q in range(focal):
            out_ref[q, r:r + 1, :] = windowed[q:q + 1]


def per_device(line, across, response, focusing, window_onset, window_end):
    _, freqs, rows, sources = response.shape
    focal, depth = focusing.shape[2], focusing.shape[3]
    per = LANES // (2 * focal)
    groups = freqs // per
    owned = rows // across
    lent, extra = divmod(lent_freqs(line, freqs, rows, focal), per)
    extra = extra if lent else 0
    kept = groups - lent
    batch = ([(lent, kept - 1)] if extra else []) + [(i, kept + i) for i in range(lent - 1)]
    slots, sent = lent + 1, max(len(batch), 1)
    tables = make_tables(across, groups, per)
    dma = pltpu.SemaphoreType.DMA
    return pl.pallas_call(
        functools.partial(spectra_kernel, line, across, lent, extra, batch),
        out_shape=pltpu.VMEM((focal, owned, NT), jnp.float32),
        in_specs=[pl.BlockSpec(memory_space=pl.ANY)] * 5,
        out_specs=pl.BlockSpec(memory_space=pltpu.VMEM),
        scratch_shapes=[
            pltpu.VMEM(response.shape, jnp.bfloat16),
            pltpu.VMEM(focusing.shape, jnp.float32),
            pltpu.VMEM((line, freqs, 2 * focal, depth), jnp.bfloat16),
            pltpu.VMEM((slots, 2, per, rows, depth), jnp.bfloat16),
            pltpu.VMEM((groups, 2 * rows, LANES), jnp.float32),
            pltpu.VMEM((slots, rows, LANES), jnp.float32),
            pltpu.VMEM((across, sent * owned, LANES), jnp.float32),
            pltpu.VMEM((across, sent * owned, LANES), jnp.float32),
            pltpu.VMEM((across, owned, LANES), jnp.float32),
            pltpu.VMEM((across, owned, LANES), jnp.float32),
            pltpu.VMEM(tables.shape, jnp.bfloat16),
            pltpu.VMEM((owned, focal), jnp.int32),
            pltpu.VMEM((owned, focal), jnp.int32),
            pltpu.VMEM((owned * focal, NT), jnp.float32),
            pltpu.VMEM((across, (groups - 1) * owned, LANES), jnp.float32),
            pltpu.VMEM((across, (groups - 1) * owned, LANES), jnp.float32),
            pltpu.VMEM((owned, groups - 1, across, LANES), jnp.float32),
            pltpu.VMEM((across, owned, LANES), jnp.float32),
            pltpu.VMEM((across, owned, LANES), jnp.float32),
            pltpu.VMEM((owned, 1, across, LANES), jnp.float32),
            pltpu.VMEM((owned, sent, across, LANES), jnp.float32),
            dma((groups,)),
            dma((groups,)),
            dma,
            dma,
            dma,
            dma((2, max(line - 1, 1), groups)),
            dma((line, groups)),
            dma((2, per)),
            dma((2, per)),
            dma((slots + per,)),
            dma((slots + per,)),
            dma((2, across)),
            dma((2, across)),
            dma((2, across)),
            dma((2, across)),
            dma((2,)),
        ],
        compiler_params=pltpu.CompilerParams(
            collective_id=0, has_side_effects=True, vmem_limit_bytes=60000 * 1024
        ),
    )(response, focusing, tables, window_onset.T, window_end.T)


def solution(mesh):
    line, across = mesh.shape["recv"], mesh.shape["freq"]
    in_specs = (
        P(None, "freq", "recv", None),
        P(None, "freq", None, "recv"),
        P(None, ("recv", "freq")),
        P(None, ("recv", "freq")),
    )
    out_specs = P(None, ("recv", "freq"), None)
    return jax.shard_map(
        functools.partial(per_device, line, across),
        mesh=mesh, in_specs=in_specs, out_specs=out_specs, check_vma=False,
    )
```

```python
import functools
import math

import jax
import jax.numpy as jnp
import numpy as np
from jax import lax
from jax.experimental import pallas as pl
from jax.experimental.pallas import tpu as pltpu
from jax.sharding import PartitionSpec as P

NT = 1024
LANES = 128
MESH = pl.DeviceIdType.MESH


def make_tables(across, groups, per, order):
    freqs = groups * per
    count = across * freqs
    phase = (np.arange(count)[:, None] * np.arange(NT)[None, :] % NT) * (2.0 * math.pi / NT)
    scale = 1.0 / math.sqrt(count)
    table = np.stack([np.cos(phase) * scale, -np.sin(phase) * scale], 1)
    table = table.reshape(across, groups, per, 2, NT)[:, order].transpose(1, 2, 3, 0, 4).reshape(-1, NT)
    high = table.astype(np.float32).astype(jnp.bfloat16)
    low = (table - high.astype(np.float64)).astype(np.float32).astype(jnp.bfloat16)
    return np.stack([high, low])


def lent_freqs(line, freqs, rows, focal, per):
    if line < 4:
        return 0
    even = (line - 2) * freqs * focal // ((line - 1) * (focal + rows))
    return max(min(even, freqs - 2 * per), 0)


def spectra_kernel(
    line, across, lent, order, tail, resp_hbm, focus_hbm, table_hbm, onset_hbm, end_hbm, out_ref,
    resp, focus, held, guest, acc, back_out, back_in, last_out, last_in, table, onset, finale, traces,
    early_out, early_in, early_rows, late_out, late_in, late_rows,
    resp_sem, focus_sem, table_sem, onset_sem, finale_sem, send_sem, recv_sem, fine_send, fine_recv,
    guest_send, guest_recv, back_send, back_recv, x_send, x_recv, x_local,
):
    me = lax.axis_index("recv")
    mine = lax.axis_index("freq")
    _, freqs, rows, _ = resp_hbm.shape
    focal, depth = focus_hbm.shape[2], focus_hbm.shape[3]
    groups = acc.shape[0]
    per = freqs // groups
    owned = rows // across
    gone, extra = divmod(lent, per)
    slots = gone + 1 if extra else gone
    early_groups, late_groups = order[:groups - tail], order[groups - tail:]
    has_left, has_right = me > 0, me < line - 1
    is_first, is_last = me == 0, me == line - 1
    left, right = jnp.maximum(me - 1, 0), jnp.minimum(me + 1, line - 1)
    is_end = is_first | is_last
    is_host = (me == 1) | (me == line - 2)
    beside_end = jnp.where(is_first, right, left)
    end = jnp.where(me == 1, 0, line - 1)
    skipped = jnp.where(is_first | (me == 1), 1, 0)

    def load_focus(g):
        return pltpu.make_async_copy(
            focus_hbm.at[:, pl.ds(g * per, per)], focus.at[:, pl.ds(g * per, per)], focus_sem.at[g]
        )

    def load_resp(g):
        return pltpu.make_async_copy(
            resp_hbm.at[:, pl.ds(g * per, per)], resp.at[:, pl.ds(g * per, per)], resp_sem.at[g]
        )

    barrier = pltpu.get_barrier_semaphore()

    @pl.when(has_left)
    def _():
        pl.semaphore_signal(barrier, inc=1, device_id={"recv": left}, device_id_type=MESH)

    @pl.when(has_right)
    def _():
        pl.semaphore_signal(barrier, inc=1, device_id={"recv": right}, device_id_type=MESH)

    for hop in range(1, across):
        other = lax.rem(mine + hop, across)
        pl.semaphore_signal(barrier, inc=1, device_id={"freq": other}, device_id_type=MESH)

    for g in range(groups):
        load_focus(g).start()
    for g in range(groups):
        load_resp(g).start()

    load_table = pltpu.make_async_copy(table_hbm, table, table_sem)
    load_table.start()
    load_onset = pltpu.make_async_copy(onset_hbm, onset, onset_sem)
    load_onset.start()
    load_finale = pltpu.make_async_copy(end_hbm, finale, finale_sem)
    load_finale.start()

    def convert(g):
        load_focus(g).wait()
        for i in range(per):
            k = g * per + i
            for part in range(2):
                held[me, k, part * focal:(part + 1) * focal, :] = focus[part, k].astype(jnp.bfloat16)

    for g in range(min(2, groups)):
        convert(g)

    beside = has_left.astype(jnp.int32) + has_right.astype(jnp.int32)
    pl.semaphore_wait(barrier, across - 1 + beside)

    def hand_on(way, step, block, g, target):
        piece = held.at[block, pl.ds(g * per, per)]
        return pltpu.make_async_remote_copy(
            src_ref=piece, dst_ref=piece,
            send_sem=send_sem.at[way, step, g], recv_sem=recv_sem.at[block, g],
            device_id={"recv": target}, device_id_type=MESH,
        )

    def hand_part(way, step, block, target):
        piece = held.at[block, pl.ds(lent, per - extra)]
        return pltpu.make_async_remote_copy(
            src_ref=piece, dst_ref=piece,
            send_sem=send_sem.at[way, step, gone], recv_sem=recv_sem.at[block, gone],
            device_id={"recv": target}, device_id_type=MESH,
        )

    def hand_last(way, block, n, target):
        piece = held.at[block, pl.ds((groups - 1) * per + n, 1)]
        return pltpu.make_async_remote_copy(
            src_ref=piece, dst_ref=piece,
            send_sem=fine_send.at[way, n], recv_sem=fine_recv.at[way, n],
            device_id={"recv": target}, device_id_type=MESH,
        )

    def pass_on(way, step, block, g, target, act):
        to_end = (me == line - 2) if way == 0 else (me == 1)
        last = to_end & (step == line - 2) & (g == groups - 1)
        part = to_end & (g == gone) if extra else False
        plain = jnp.logical_not(last | part | (to_end & (g < gone)))

        @pl.when(plain)
        def _():
            act(hand_on(way, step, block, g, target))

        @pl.when(last)
        def _():
            for n in range(per):
                act(hand_last(way, block, n, target))

        if extra:
            @pl.when(part)
            def _():
                act(hand_part(way, step, block, target))

    def lend(k, target):
        columns = pl.ds(pl.multiple_of(skipped * depth, LANES), (line - 1) * depth)
        return pltpu.make_async_remote_copy(
            src_ref=resp.at[:, k, :, columns], dst_ref=guest.at[k],
            send_sem=guest_send.at[k], recv_sem=guest_recv.at[k],
            device_id={"recv": target}, device_id_type=MESH,
        )

    def lend_last(n, target):
        columns = pl.ds(pl.multiple_of((n + skipped) * depth, LANES), depth)
        return pltpu.make_async_remote_copy(
            src_ref=resp.at[:, lent - 1, :, columns],
            dst_ref=guest.at[lent - 1, :, :, pl.ds(n * depth, depth)],
            send_sem=guest_send.at[lent - 1 + n], recv_sem=guest_recv.at[lent - 1 + n],
            device_id={"recv": target}, device_id_type=MESH,
        )

    def give_back(part, source, target, place):
        copies = []
        for other in range(across):
            copies.append(pltpu.make_async_remote_copy(
                src_ref=source.at[other], dst_ref=target.at[mine],
                send_sem=back_send.at[part, other], recv_sem=back_recv.at[part, mine],
                device_id={"recv": place, "freq": other}, device_id_type=MESH,
            ))
        return copies

    def take_back(part, source, target, place):
        copies = []
        for other in range(across):
            copies.append(pltpu.make_async_remote_copy(
                src_ref=source.at[other], dst_ref=target.at[other],
                send_sem=back_send.at[part, other], recv_sem=back_recv.at[part, other],
                device_id={"recv": place, "freq": other}, device_id_type=MESH,
            ))
        return copies

    @pl.loop(0, groups)
    def _(g):
        @pl.when(has_right)
        def _():
            pass_on(0, 0, me, g, right, lambda copy: copy.start())

        @pl.when(has_left)
        def _():
            pass_on(1, 0, me, g, left, lambda copy: copy.start())

        @pl.when(g + 2 < groups)
        def _():
            convert(g + 2)

    def multiply(lhs, rhs):
        return lax.dot_general(
            lhs.reshape(2 * rows, depth), rhs, (((1,), (1,)), ((), ())),
            preferred_element_type=jnp.float32,
        )

    def of_block(block, g, first=0):
        columns = pl.ds(pl.multiple_of(block * depth, LANES), depth)
        parts = [jnp.zeros((2 * rows, 2 * focal), jnp.float32)] * first
        for k in range(first, per):
            parts.append(multiply(resp[:, g * per + k, :, columns], held[block, g * per + k]))
        return jnp.concatenate(parts, axis=1)

    @pl.loop(0, groups)
    def _(g):
        load_resp(g).wait()

    if lent:
        @pl.when(is_end)
        def _():
            for k in range(lent - 1):
                lend(k, beside_end).start()
            for n in range(line - 1):
                lend_last(n, beside_end).start()

    @pl.loop(0, groups)
    def _(g):
        acc[g] = of_block(me, g)

    half = lax.rem(lax.broadcasted_iota(jnp.int32, (rows, LANES), 1), 2 * focal) < focal

    def combine(tile):
        real, imag = tile[:rows], tile[rows:]
        return real + jnp.where(
            half, -pltpu.roll(imag, LANES - focal, axis=1), pltpu.roll(imag, focal, axis=1)
        )

    def serve(slot):
        parts = []
        for k in range(slot * per, (slot + 1) * per):
            if k >= lent:
                parts.append(jnp.zeros((2 * rows, 2 * focal), jnp.float32))
                continue
            if k < lent - 1:
                lend(k, end).wait_recv()
            total = None
            for n in range(line - 1):
                if k == lent - 1:
                    lend_last(n, end).wait_recv()
                term = multiply(guest[k, :, :, n * depth:(n + 1) * depth], held[n + skipped, k])
                total = term if total is None else total + term
            parts.append(total)
        return combine(jnp.concatenate(parts, axis=1))

    def split_rows(tile, at, target):
        for d in range(across):
            target[d, at * owned:(at + 1) * owned, :] = tile[d * owned:(d + 1) * owned]

    def visit(t):
        step, g = 1 + t // groups, t % groups
        from_left, from_right = me - step, me + step
        due_left, due_right = from_left >= 0, from_right < line
        if lent:
            wanted = jnp.logical_not(is_end) | (g >= gone)
            due_left, due_right = due_left & wanted, due_right & wanted
        if extra:
            part = is_end & (g == gone)
            due_left, due_right = due_left & jnp.logical_not(part), due_right & jnp.logical_not(part)

            @pl.when(part)
            def _():
                block = jnp.where(is_first, from_right, from_left)
                hand_part(jnp.where(is_first, 1, 0), 0, block, beside_end).wait_recv()
                acc[gone] = acc[gone] + of_block(block, gone, extra)

        left_block, right_block = jnp.maximum(from_left, 0), jnp.minimum(from_right, line - 1)

        @pl.when(due_left)
        def _():
            hand_on(0, 0, left_block, g, left).wait_recv()

            @pl.when(has_right & (step < line - 1))
            def _():
                pass_on(0, step, left_block, g, right, lambda copy: copy.start())

        @pl.when(due_right)
        def _():
            hand_on(1, 0, right_block, g, right).wait_recv()

            @pl.when(has_left & (step < line - 1))
            def _():
                pass_on(1, step, right_block, g, left, lambda copy: copy.start())

        @pl.loop(0, 2)
        def _(side):
            @pl.when(((side == 0) & due_left) | ((side == 1) & due_right))
            def _():
                acc[g] = acc[g] + of_block(jnp.where(side == 0, left_block, right_block), g)

        if slots > 1:
            @pl.when(is_host & (step == line - 2) & (g == groups - 2))
            def _():
                for slot in range(slots - 1):
                    split_rows(serve(slot), slot, back_out)
                for copy in give_back(0, back_out, back_in, end):
                    copy.start()

    def visit_end():
        @pl.when(is_end)
        def _():
            block = jnp.where(is_first, line - 1, 0)
            columns = pl.ds(pl.multiple_of(block * depth, LANES), depth)
            parts = []
            for n in range(per):
                hand_last(jnp.where(is_first, 1, 0), block, n, beside_end).wait_recv()
                k = (groups - 1) * per + n
                parts.append(multiply(resp[:, k, :, columns], held[block, k]))
            acc[groups - 1] = acc[groups - 1] + jnp.concatenate(parts, axis=1)

    @pl.loop(0, (line - 1) * groups - tail)
    def _(t):
        visit(t)

    def exchange(part, source, target):
        copies = []
        for hop in range(1, across):
            other = lax.rem(mine + hop, across)
            copies.append(pltpu.make_async_remote_copy(
                src_ref=source.at[other], dst_ref=target.at[mine],
                send_sem=x_send.at[part, hop], recv_sem=x_recv.at[part, hop],
                device_id={"freq": other}, device_id_type=MESH,
            ))
        copies.append(pltpu.make_async_copy(source.at[mine], target.at[mine], x_local.at[part]))
        return copies

    def arrange(source, count, target, at, add=False):
        for f in range(across):
            for r in range(owned):
                lines = source[f, pl.ds(r, count, stride=owned), :] if count > 1 else source[f, r:r + 1, :]
                for g in range(count):
                    value = lines[g:g + 1]
                    if add:
                        value = value + target[r, at + g, f:f + 1, :]
                    target[r, at + g, f:f + 1, :] = value

    def transform(source, place):
        parts = []
        for g in range(source.shape[1]):
            for m in range(2 * per):
                lanes = [source[r, g, :, m * focal:(m + 1) * focal] for r in range(owned)]
                parts.append(jnp.concatenate(lanes, axis=1))
        values = jnp.concatenate(parts, axis=0)
        high = values.astype(jnp.bfloat16)
        low = (values - high.astype(jnp.float32)).astype(jnp.bfloat16)
        first = place * 2 * per * across
        span = slice(first, first + values.shape[0])

        def dot(a, b):
            return lax.dot_general(a, b, (((0,), (0,)), ((), ())), preferred_element_type=jnp.float32)

        return dot(high, table[0, span]) + (dot(low, table[0, span]) + dot(high, table[1, span]))

    for at, g in enumerate(early_groups):
        split_rows(combine(acc[g]), at, early_out)
    early = exchange(0, early_out, early_in)
    for copy in early:
        copy.start()
    if slots:
        late_rows[:, 0] = jnp.zeros((owned, across, LANES), jnp.float32)
    for t in range((line - 1) * groups - tail, (line - 1) * groups - 1):
        visit(t)
    load_table.wait()
    load_onset.wait()
    load_finale.wait()
    for copy in early:
        copy.wait()
    arrange(early_in, len(early_groups), early_rows, 0)
    if slots > 1:
        @pl.when(is_end)
        def _():
            for copy in take_back(0, back_out, back_in, beside_end):
                copy.wait_recv()
            arrange(back_in, slots - 1, early_rows, 0, True)

    traces[...] = transform(early_rows, 0)
    visit_end()

    for at, g in enumerate(late_groups):
        split_rows(combine(acc[g]), at, late_out)
    late = exchange(1, late_out, late_in)
    for copy in late:
        copy.start()

    if slots:
        @pl.when(is_host)
        def _():
            split_rows(serve(slots - 1), 0, last_out)
            for copy in give_back(1, last_out, last_in, end):
                copy.start()

    @pl.loop(0, (line - 1) * groups)
    def _(t):
        step, g = t // groups, t % groups

        @pl.when(has_right & (me - step >= 0))
        def _():
            pass_on(0, step, me, g, right, lambda copy: copy.wait_send())

        @pl.when(has_left & (me + step < line))
        def _():
            pass_on(1, step, me, g, left, lambda copy: copy.wait_send())

    if slots:
        @pl.when(is_end)
        def _():
            for k in range(lent - 1):
                lend(k, beside_end).wait_send()
            for n in range(line - 1):
                lend_last(n, beside_end).wait_send()

        @pl.when(is_host)
        def _():
            if slots > 1:
                for copy in give_back(0, back_out, back_in, end):
                    copy.wait_send()
            for copy in give_back(1, last_out, last_in, end):
                copy.wait_send()

    samples = lax.broadcasted_iota(jnp.int32, (focal, NT), 1)
    starts, ends = jnp.transpose(onset[...]), jnp.transpose(finale[...])
    for copy in late:
        copy.wait()
    arrange(late_in, tail, late_rows, 1 if slots else 0)
    if slots:
        @pl.when(is_end)
        def _():
            for copy in take_back(1, last_out, last_in, beside_end):
                copy.wait_recv()
            arrange(last_in, 1, late_rows, 0)

    total = traces[...] + transform(late_rows, groups - late_rows.shape[1])
    for r in range(owned):
        inside = (samples >= starts[:, r:r + 1]) & (samples < ends[:, r:r + 1])
        windowed = jnp.where(inside, total[r * focal:(r + 1) * focal], 0.0)
        for q in range(focal):
            out_ref[q, r:r + 1, :] = windowed[q:q + 1]


def per_device(line, across, response, focusing, window_onset, window_end):
    _, freqs, rows, sources = response.shape
    focal, depth = focusing.shape[2], focusing.shape[3]
    per = LANES // (2 * focal)
    groups = freqs // per
    owned = rows // across
    tail = min(2, groups - 1)
    lent = lent_freqs(line, freqs, rows, focal, per)
    slots = -(-lent // per)
    near = [slots - 1] if slots else []
    order = [g for g in range(groups - tail) if g not in near] + near + list(range(groups - tail, groups))
    sent = max(slots - 1, 1)
    tables = make_tables(across, groups, per, order)
    dma = pltpu.SemaphoreType.DMA
    return pl.pallas_call(
        functools.partial(spectra_kernel, line, across, lent, order, tail),
        out_shape=pltpu.VMEM((focal, owned, NT), jnp.float32),
        in_specs=[pl.BlockSpec(memory_space=pl.ANY)] * 5,
        out_specs=pl.BlockSpec(memory_space=pltpu.VMEM),
        scratch_shapes=[
            pltpu.VMEM(response.shape, jnp.bfloat16),
            pltpu.VMEM(focusing.shape, jnp.float32),
            pltpu.VMEM((line, freqs, 2 * focal, depth), jnp.bfloat16),
            pltpu.VMEM((max(lent, 1), 2, rows, (line - 1) * depth), jnp.bfloat16),
            pltpu.VMEM((groups, 2 * rows, LANES), jnp.float32),
            pltpu.VMEM((across, sent * owned, LANES), jnp.float32),
            pltpu.VMEM((across, sent * owned, LANES), jnp.float32),
            pltpu.VMEM((across, owned, LANES), jnp.float32),
            pltpu.VMEM((across, owned, LANES), jnp.float32),
            pltpu.VMEM(tables.shape, jnp.bfloat16),
            pltpu.VMEM((owned, focal), jnp.int32),
            pltpu.VMEM((owned, focal), jnp.int32),
            pltpu.VMEM((owned * focal, NT), jnp.float32),
            pltpu.VMEM((across, (groups - tail) * owned, LANES), jnp.float32),
            pltpu.VMEM((across, (groups - tail) * owned, LANES), jnp.float32),
            pltpu.VMEM((owned, groups - tail, across, LANES), jnp.float32),
            pltpu.VMEM((across, tail * owned, LANES), jnp.float32),
            pltpu.VMEM((across, tail * owned, LANES), jnp.float32),
            pltpu.VMEM((owned, tail + len(near), across, LANES), jnp.float32),
            dma((groups,)),
            dma((groups,)),
            dma,
            dma,
            dma,
            dma((2, max(line - 1, 1), groups)),
            dma((line, groups)),
            dma((2, per)),
            dma((2, per)),
            dma((lent + line,)),
            dma((lent + line,)),
            dma((2, across)),
            dma((2, across)),
            dma((2, across)),
            dma((2, across)),
            dma((2,)),
        ],
        compiler_params=pltpu.CompilerParams(
            collective_id=0, has_side_effects=True, vmem_limit_bytes=60000 * 1024
        ),
    )(response, focusing, tables, window_onset.T, window_end.T)


def solution(mesh):
    line, across = mesh.shape["recv"], mesh.shape["freq"]
    in_specs = (
        P(None, "freq", "recv", None),
        P(None, "freq", None, "recv"),
        P(None, ("recv", "freq")),
        P(None, ("recv", "freq")),
    )
    out_specs = P(None, ("recv", "freq"), None)
    return jax.shard_map(
        functools.partial(per_device, line, across),
        mesh=mesh, in_specs=in_specs, out_specs=out_specs, check_vma=False,
    )
```

```python
import functools
import math

import jax
import jax.numpy as jnp
import numpy as np
from jax import lax
from jax.experimental import pallas as pl
from jax.experimental.pallas import tpu as pltpu
from jax.sharding import PartitionSpec as P

NT = 1024
LANES = 128
MESH = pl.DeviceIdType.MESH


def make_tables(across, groups, per):
    freqs = groups * per
    count = across * freqs
    phase = (np.arange(count)[:, None] * np.arange(NT)[None, :] % NT) * (2.0 * math.pi / NT)
    scale = 1.0 / math.sqrt(count)
    table = np.stack([np.cos(phase) * scale, -np.sin(phase) * scale], 1)
    table = table.reshape(across, groups, per, 2, NT).transpose(1, 2, 3, 0, 4).reshape(-1, NT)
    high = table.astype(np.float32).astype(jnp.bfloat16)
    low = (table - high.astype(np.float64)).astype(np.float32).astype(jnp.bfloat16)
    return np.stack([high, low])


def lent_freqs(line, freqs, rows, focal, per):
    if line < 4:
        return 0
    even = (line - 2) * freqs * focal // ((line - 1) * (focal + rows))
    return max(min(even, freqs - per), 0)


def spectra_kernel(
    line, across, lent, resp_hbm, focus_hbm, table_hbm, onset_hbm, end_hbm, out_ref,
    resp, focus, held, guest, acc, back_out, back_in, table, onset, finale, traces,
    early_out, early_in, late_out, late_in,
    resp_sem, focus_sem, table_sem, onset_sem, finale_sem, send_sem, recv_sem, fine_send, fine_recv,
    guest_send, guest_recv, back_send, back_recv, x_send, x_recv, x_local,
):
    me = lax.axis_index("recv")
    mine = lax.axis_index("freq")
    _, freqs, rows, _ = resp_hbm.shape
    focal, depth = focus_hbm.shape[2], focus_hbm.shape[3]
    groups = acc.shape[0]
    per = freqs // groups
    owned = rows // across
    slots = -(-lent // per)
    mixed = groups - 1 - slots
    extra = lent % per
    gone = mixed + 1 if extra else mixed
    first_lent = (groups - 1) * per - lent
    has_left, has_right = me > 0, me < line - 1
    is_first, is_last = me == 0, me == line - 1
    left, right = jnp.maximum(me - 1, 0), jnp.minimum(me + 1, line - 1)
    is_end = is_first | is_last
    is_host = (me == 1) | (me == line - 2)
    beside_end = jnp.where(is_first, right, left)
    end = jnp.where(me == 1, 0, line - 1)
    skipped = jnp.where(is_first | (me == 1), 1, 0)

    def load_focus(g):
        return pltpu.make_async_copy(
            focus_hbm.at[:, pl.ds(g * per, per)], focus.at[:, pl.ds(g * per, per)], focus_sem.at[g]
        )

    def load_resp(g):
        return pltpu.make_async_copy(
            resp_hbm.at[:, pl.ds(g * per, per)], resp.at[:, pl.ds(g * per, per)], resp_sem.at[g]
        )

    for g in range(groups):
        load_focus(g).start()

    barrier = pltpu.get_barrier_semaphore()

    @pl.when(has_left)
    def _():
        pl.semaphore_signal(barrier, inc=1, device_id={"recv": left}, device_id_type=MESH)

    @pl.when(has_right)
    def _():
        pl.semaphore_signal(barrier, inc=1, device_id={"recv": right}, device_id_type=MESH)

    for hop in range(1, across):
        other = lax.rem(mine + hop, across)
        pl.semaphore_signal(barrier, inc=1, device_id={"freq": other}, device_id_type=MESH)

    for g in range(groups):
        load_resp(g).start()

    load_table = pltpu.make_async_copy(table_hbm, table, table_sem)
    load_table.start()
    load_onset = pltpu.make_async_copy(onset_hbm, onset, onset_sem)
    load_onset.start()
    load_finale = pltpu.make_async_copy(end_hbm, finale, finale_sem)
    load_finale.start()

    def convert(g):
        load_focus(g).wait()
        for i in range(per):
            k = g * per + i
            for part in range(2):
                held[me, k, part * focal:(part + 1) * focal, :] = focus[part, k].astype(jnp.bfloat16)

    for g in range(min(2, groups)):
        convert(g)

    beside = has_left.astype(jnp.int32) + has_right.astype(jnp.int32)
    pl.semaphore_wait(barrier, across - 1 + beside)

    def hand_on(way, step, block, g, target):
        piece = held.at[block, pl.ds(g * per, per)]
        return pltpu.make_async_remote_copy(
            src_ref=piece, dst_ref=piece,
            send_sem=send_sem.at[way, step, g], recv_sem=recv_sem.at[block, g],
            device_id={"recv": target}, device_id_type=MESH,
        )

    def hand_part(way, step, block, target):
        piece = held.at[block, pl.ds(mixed * per, per - extra)]
        return pltpu.make_async_remote_copy(
            src_ref=piece, dst_ref=piece,
            send_sem=send_sem.at[way, step, mixed], recv_sem=recv_sem.at[block, mixed],
            device_id={"recv": target}, device_id_type=MESH,
        )

    def hand_last(way, block, n, target):
        piece = held.at[block, pl.ds((groups - 1) * per + n, 1)]
        return pltpu.make_async_remote_copy(
            src_ref=piece, dst_ref=piece,
            send_sem=fine_send.at[way, n], recv_sem=fine_recv.at[way, n],
            device_id={"recv": target}, device_id_type=MESH,
        )

    def pass_on(way, step, block, g, target, act):
        to_end = (me == line - 2) if way == 0 else (me == 1)
        last = to_end & (step == line - 2) & (g == groups - 1)
        part = to_end & (g == mixed) if extra else False
        plain = jnp.logical_not(last | part | (to_end & (g >= gone) & (g < groups - 1)))

        @pl.when(plain)
        def _():
            act(hand_on(way, step, block, g, target))

        @pl.when(last)
        def _():
            for n in range(per):
                act(hand_last(way, block, n, target))

        if extra:
            @pl.when(part)
            def _():
                act(hand_part(way, step, block, target))

    def lend(k, target):
        columns = pl.ds(pl.multiple_of(skipped * depth, LANES), (line - 1) * depth)
        return pltpu.make_async_remote_copy(
            src_ref=resp.at[:, first_lent + k, :, columns], dst_ref=guest.at[k],
            send_sem=guest_send.at[k], recv_sem=guest_recv.at[k],
            device_id={"recv": target}, device_id_type=MESH,
        )

    def lend_last(n, target):
        columns = pl.ds(pl.multiple_of((n + skipped) * depth, LANES), depth)
        return pltpu.make_async_remote_copy(
            src_ref=resp.at[:, (groups - 1) * per - 1, :, columns],
            dst_ref=guest.at[lent - 1, :, :, pl.ds(n * depth, depth)],
            send_sem=guest_send.at[lent - 1 + n], recv_sem=guest_recv.at[lent - 1 + n],
            device_id={"recv": target}, device_id_type=MESH,
        )

    def give_back(place):
        copies = []
        for other in range(across):
            copies.append(pltpu.make_async_remote_copy(
                src_ref=back_out.at[other], dst_ref=back_in.at[mine],
                send_sem=back_send.at[other], recv_sem=back_recv.at[mine],
                device_id={"recv": place, "freq": other}, device_id_type=MESH,
            ))
        return copies

    def take_back(place):
        copies = []
        for other in range(across):
            copies.append(pltpu.make_async_remote_copy(
                src_ref=back_out.at[other], dst_ref=back_in.at[other],
                send_sem=back_send.at[other], recv_sem=back_recv.at[other],
                device_id={"recv": place, "freq": other}, device_id_type=MESH,
            ))
        return copies

    @pl.loop(0, groups)
    def _(g):
        @pl.when(has_right)
        def _():
            pass_on(0, 0, me, g, right, lambda copy: copy.start())

        @pl.when(has_left)
        def _():
            pass_on(1, 0, me, g, left, lambda copy: copy.start())

        @pl.when(g + 2 < groups)
        def _():
            convert(g + 2)

    def multiply(lhs, rhs):
        return lax.dot_general(
            lhs.reshape(2 * rows, depth), rhs, (((1,), (1,)), ((), ())),
            preferred_element_type=jnp.float32,
        )

    def of_block(block, g, count=per):
        columns = pl.ds(pl.multiple_of(block * depth, LANES), depth)
        parts = []
        for k in range(count):
            parts.append(multiply(resp[:, g * per + k, :, columns], held[block, g * per + k]))
        parts += [jnp.zeros((2 * rows, 2 * focal), jnp.float32)] * (per - count)
        return jnp.concatenate(parts, axis=1)

    @pl.loop(0, groups)
    def _(g):
        load_resp(g).wait()

    if lent:
        @pl.when(is_end)
        def _():
            for k in range(lent - 1):
                lend(k, beside_end).start()
            for n in range(line - 1):
                lend_last(n, beside_end).start()

    @pl.loop(0, groups)
    def _(g):
        acc[g] = of_block(me, g)

    half = lax.rem(lax.broadcasted_iota(jnp.int32, (rows, LANES), 1), 2 * focal) < focal

    def combine(tile):
        real, imag = tile[:rows], tile[rows:]
        return real + jnp.where(
            half, -pltpu.roll(imag, LANES - focal, axis=1), pltpu.roll(imag, focal, axis=1)
        )

    def serve(slot):
        parts = []
        for n in range(per):
            k = lent - (slots - slot) * per + n
            if k < 0:
                parts.append(jnp.zeros((2 * rows, 2 * focal), jnp.float32))
                continue
            if k < lent - 1:
                lend(k, end).wait_recv()
            total = None
            for n in range(line - 1):
                if k == lent - 1:
                    lend_last(n, end).wait_recv()
                term = multiply(guest[k, :, :, n * depth:(n + 1) * depth], held[n + skipped, first_lent + k])
                total = term if total is None else total + term
            parts.append(total)
        return combine(jnp.concatenate(parts, axis=1))

    def split_rows(tile, at, target):
        for d in range(across):
            target[d, at * owned:(at + 1) * owned, :] = tile[d * owned:(d + 1) * owned]

    def visit(t):
        step, g = 1 + t // groups, t % groups
        from_left, from_right = me - step, me + step
        due_left, due_right = from_left >= 0, from_right < line
        if lent:
            wanted = jnp.logical_not(is_end) | (g < gone) | (g == groups - 1)
            due_left, due_right = due_left & wanted, due_right & wanted
        if extra:
            part = is_end & (g == mixed)
            due_left, due_right = due_left & jnp.logical_not(part), due_right & jnp.logical_not(part)

            @pl.when(part)
            def _():
                block = jnp.where(is_first, from_right, from_left)
                hand_part(jnp.where(is_first, 1, 0), 0, block, beside_end).wait_recv()
                acc[mixed] = acc[mixed] + of_block(block, mixed, per - extra)

        left_block, right_block = jnp.maximum(from_left, 0), jnp.minimum(from_right, line - 1)

        @pl.when(due_left)
        def _():
            hand_on(0, 0, left_block, g, left).wait_recv()

            @pl.when(has_right & (step < line - 1))
            def _():
                pass_on(0, step, left_block, g, right, lambda copy: copy.start())

        @pl.when(due_right)
        def _():
            hand_on(1, 0, right_block, g, right).wait_recv()

            @pl.when(has_left & (step < line - 1))
            def _():
                pass_on(1, step, right_block, g, left, lambda copy: copy.start())

        @pl.loop(0, 2)
        def _(side):
            @pl.when(((side == 0) & due_left) | ((side == 1) & due_right))
            def _():
                acc[g] = acc[g] + of_block(jnp.where(side == 0, left_block, right_block), g)

        if slots > 1:
            @pl.when(is_host & (step == line - 2) & (g == groups - 2))
            def _():
                for slot in range(slots - 1):
                    split_rows(serve(slot), slot, back_out)

    def visit_end():
        @pl.when(is_end)
        def _():
            block = jnp.where(is_first, line - 1, 0)
            columns = pl.ds(pl.multiple_of(block * depth, LANES), depth)
            parts = []
            for n in range(per):
                hand_last(jnp.where(is_first, 1, 0), block, n, beside_end).wait_recv()
                k = (groups - 1) * per + n
                parts.append(multiply(resp[:, k, :, columns], held[block, k]))
            acc[groups - 1] = acc[groups - 1] + jnp.concatenate(parts, axis=1)

    @pl.loop(0, (line - 1) * groups - 1)
    def _(t):
        visit(t)

    def exchange(part, source, target):
        copies = []
        for hop in range(1, across):
            other = lax.rem(mine + hop, across)
            copies.append(pltpu.make_async_remote_copy(
                src_ref=source.at[other], dst_ref=target.at[mine],
                send_sem=x_send.at[part, hop], recv_sem=x_recv.at[part, hop],
                device_id={"freq": other}, device_id_type=MESH,
            ))
        copies.append(pltpu.make_async_copy(source.at[mine], target.at[mine], x_local.at[part]))
        return copies

    def lines(source, r, g):
        return source[:, g * owned + r, :]

    def transform(pieces, place):
        parts = []
        for source, count in pieces:
            for g in range(count):
                rows_of = [lines(source, r, g) for r in range(owned)]
                for m in range(2 * per):
                    lanes = [row[:, m * focal:(m + 1) * focal] for row in rows_of]
                    parts.append(jnp.concatenate(lanes, axis=1))
        values = jnp.concatenate(parts, axis=0)
        high = values.astype(jnp.bfloat16)
        low = (values - high.astype(jnp.float32)).astype(jnp.bfloat16)
        first = place * 2 * per * across
        span = slice(first, first + values.shape[0])

        def dot(a, b):
            return lax.dot_general(a, b, (((0,), (0,)), ((), ())), preferred_element_type=jnp.float32)

        return dot(high, table[0, span]) + (dot(low, table[0, span]) + dot(high, table[1, span]))

    for g in range(groups - 1):
        split_rows(combine(acc[g]), g, early_out)
    early = exchange(0, early_out, early_in)
    for copy in early:
        copy.start()
    if slots:
        @pl.when(jnp.logical_not(is_end))
        def _():
            back_in[...] = jnp.zeros_like(back_in)

    load_table.wait()
    load_onset.wait()
    load_finale.wait()
    for copy in early:
        copy.wait()
    traces[...] = transform([(early_in, groups - 1)], 0)
    visit_end()

    split_rows(combine(acc[groups - 1]), 0, late_out)
    late = exchange(1, late_out, late_in)
    for copy in late:
        copy.start()

    if slots:
        @pl.when(is_host)
        def _():
            split_rows(serve(slots - 1), slots - 1, back_out)
            for copy in give_back(end):
                copy.start()

    @pl.loop(0, (line - 1) * groups)
    def _(t):
        step, g = t // groups, t % groups

        @pl.when(has_right & (me - step >= 0))
        def _():
            pass_on(0, step, me, g, right, lambda copy: copy.wait_send())

        @pl.when(has_left & (me + step < line))
        def _():
            pass_on(1, step, me, g, left, lambda copy: copy.wait_send())

    if slots:
        @pl.when(is_end)
        def _():
            for k in range(lent - 1):
                lend(k, beside_end).wait_send()
            for n in range(line - 1):
                lend_last(n, beside_end).wait_send()

        @pl.when(is_host)
        def _():
            for copy in give_back(end):
                copy.wait_send()

    samples = lax.broadcasted_iota(jnp.int32, (focal, NT), 1)
    starts, ends = jnp.transpose(onset[...]), jnp.transpose(finale[...])
    for copy in late:
        copy.wait()
    late_pieces = [(late_in, 1)]
    if slots:
        late_pieces = [(back_in, slots)] + late_pieces

        @pl.when(is_end)
        def _():
            for copy in take_back(beside_end):
                copy.wait_recv()

    total = traces[...] + transform(late_pieces, groups - 1 - slots)
    for r in range(owned):
        inside = (samples >= starts[:, r:r + 1]) & (samples < ends[:, r:r + 1])
        windowed = jnp.where(inside, total[r * focal:(r + 1) * focal], 0.0)
        out_ref[:, r, :] = windowed


def per_device(line, across, response, focusing, window_onset, window_end):
    _, freqs, rows, sources = response.shape
    focal, depth = focusing.shape[2], focusing.shape[3]
    per = LANES // (2 * focal)
    groups = freqs // per
    owned = rows // across
    lent = lent_freqs(line, freqs, rows, focal, per)
    slots = -(-lent // per)
    early_lines, late_lines, back_lines = (-(-count * owned // 8) * 8 for count in (groups - 1, 1, max(slots, 1)))
    tables = make_tables(across, groups, per)
    dma = pltpu.SemaphoreType.DMA
    return pl.pallas_call(
        functools.partial(spectra_kernel, line, across, lent),
        out_shape=pltpu.VMEM((focal, owned, NT), jnp.float32),
        in_specs=[pl.BlockSpec(memory_space=pl.ANY)] * 5,
        out_specs=pl.BlockSpec(memory_space=pltpu.VMEM),
        scratch_shapes=[
            pltpu.VMEM(response.shape, jnp.bfloat16),
            pltpu.VMEM(focusing.shape, jnp.float32),
            pltpu.VMEM((line, freqs, 2 * focal, depth), jnp.bfloat16),
            pltpu.VMEM((max(lent, 1), 2, rows, (line - 1) * depth), jnp.bfloat16),
            pltpu.VMEM((groups, 2 * rows, LANES), jnp.float32),
            pltpu.VMEM((across, back_lines, LANES), jnp.float32),
            pltpu.VMEM((across, back_lines, LANES), jnp.float32),
            pltpu.VMEM(tables.shape, jnp.bfloat16),
            pltpu.VMEM((owned, focal), jnp.int32),
            pltpu.VMEM((owned, focal), jnp.int32),
            pltpu.VMEM((owned * focal, NT), jnp.float32),
            pltpu.VMEM((across, early_lines, LANES), jnp.float32),
            pltpu.VMEM((across, early_lines, LANES), jnp.float32),
            pltpu.VMEM((across, late_lines, LANES), jnp.float32),
            pltpu.VMEM((across, late_lines, LANES), jnp.float32),
            dma((groups,)),
            dma((groups,)),
            dma,
            dma,
            dma,
            dma((2, max(line - 1, 1), groups)),
            dma((line, groups)),
            dma((2, per)),
            dma((2, per)),
            dma((lent + line,)),
            dma((lent + line,)),
            dma((across,)),
            dma((across,)),
            dma((2, across)),
            dma((2, across)),
            dma((2,)),
        ],
        compiler_params=pltpu.CompilerParams(
            collective_id=0, has_side_effects=True, vmem_limit_bytes=60000 * 1024
        ),
    )(response, focusing, tables, window_onset.T, window_end.T)


def solution(mesh):
    line, across = mesh.shape["recv"], mesh.shape["freq"]
    in_specs = (
        P(None, "freq", "recv", None),
        P(None, "freq", None, "recv"),
        P(None, ("recv", "freq")),
        P(None, ("recv", "freq")),
    )
    out_specs = P(None, ("recv", "freq"), None)
    return jax.shard_map(
        functools.partial(per_device, line, across),
        mesh=mesh, in_specs=in_specs, out_specs=out_specs, check_vma=False,
    )
```

```python
import functools
import math

import jax
import jax.numpy as jnp
import numpy as np
from jax import lax
from jax.experimental import pallas as pl
from jax.experimental.pallas import tpu as pltpu
from jax.sharding import PartitionSpec as P

NT = 1024
LANES = 128
MESH = pl.DeviceIdType.MESH


def make_tables(across, groups, per):
    freqs = groups * per
    count = across * freqs
    phase = (np.arange(count)[:, None] * np.arange(NT)[None, :] % NT) * (2.0 * math.pi / NT)
    scale = 1.0 / math.sqrt(count)
    table = np.stack([np.cos(phase) * scale, -np.sin(phase) * scale], 1)
    table = table.reshape(across, groups, per, 2, NT).transpose(1, 2, 3, 0, 4).reshape(-1, NT)
    high = table.astype(np.float32).astype(jnp.bfloat16)
    low = (table - high.astype(np.float64)).astype(np.float32).astype(jnp.bfloat16)
    return np.stack([high, low])


def lent_freqs(line, freqs, rows, focal, per):
    if line < 4:
        return 0
    even = (line - 2) * freqs * focal // ((line - 1) * (focal + rows))
    return max(min(even, freqs - per), 0)


def lent_sources(line, freqs, rows, focal, per, lent, depth):
    if lent % per != per - 1:
        return 0
    even = (line - 2) * freqs * focal * depth // (focal + rows) - (line - 1) * lent * depth
    return min(-(-even // LANES) * LANES, depth - LANES)


def spectra_kernel(
    line, across, lent, cols, resp_hbm, focus_hbm, table_hbm, onset_hbm, end_hbm, out_ref,
    resp, focus, held, guest, morsel, acc, back_out, back_in, table, onset, finale, traces,
    early_out, early_in, late_out, late_in,
    resp_sem, focus_sem, table_sem, onset_sem, finale_sem, send_sem, recv_sem, fine_send, fine_recv,
    guest_send, guest_recv, back_send, back_recv, x_send, x_recv, x_local,
):
    me = lax.axis_index("recv")
    mine = lax.axis_index("freq")
    _, freqs, rows, _ = resp_hbm.shape
    focal, depth = focus_hbm.shape[2], focus_hbm.shape[3]
    groups = acc.shape[0]
    per = freqs // groups
    owned = rows // across
    slots = -(-lent // per)
    mixed = groups - 1 - slots
    extra = lent % per
    gone = mixed + 1 if extra else mixed
    first_lent = (groups - 1) * per - lent
    has_left, has_right = me > 0, me < line - 1
    is_first, is_last = me == 0, me == line - 1
    left, right = jnp.maximum(me - 1, 0), jnp.minimum(me + 1, line - 1)
    is_end = is_first | is_last
    is_host = (me == 1) | (me == line - 2)
    beside_end = jnp.where(is_first, right, left)
    end = jnp.where(me == 1, 0, line - 1)
    skipped = jnp.where(is_first | (me == 1), 1, 0)

    def load_focus(g):
        return pltpu.make_async_copy(
            focus_hbm.at[:, pl.ds(g * per, per)], focus.at[:, pl.ds(g * per, per)], focus_sem.at[g]
        )

    def load_resp(g):
        return pltpu.make_async_copy(
            resp_hbm.at[:, pl.ds(g * per, per)], resp.at[:, pl.ds(g * per, per)], resp_sem.at[g]
        )

    for g in range(groups):
        load_focus(g).start()

    barrier = pltpu.get_barrier_semaphore()

    @pl.when(has_left)
    def _():
        pl.semaphore_signal(barrier, inc=1, device_id={"recv": left}, device_id_type=MESH)

    @pl.when(has_right)
    def _():
        pl.semaphore_signal(barrier, inc=1, device_id={"recv": right}, device_id_type=MESH)

    for hop in range(1, across):
        other = lax.rem(mine + hop, across)
        pl.semaphore_signal(barrier, inc=1, device_id={"freq": other}, device_id_type=MESH)

    for g in range(groups):
        load_resp(g).start()

    load_table = pltpu.make_async_copy(table_hbm, table, table_sem)
    load_table.start()
    load_onset = pltpu.make_async_copy(onset_hbm, onset, onset_sem)
    load_onset.start()
    load_finale = pltpu.make_async_copy(end_hbm, finale, finale_sem)
    load_finale.start()

    def convert(g):
        load_focus(g).wait()
        for i in range(per):
            k = g * per + i
            for part in range(2):
                held[me, k, part * focal:(part + 1) * focal, :] = focus[part, k].astype(jnp.bfloat16)

    for g in range(min(2, groups)):
        convert(g)

    beside = has_left.astype(jnp.int32) + has_right.astype(jnp.int32)
    pl.semaphore_wait(barrier, across - 1 + beside)

    def hand_on(way, step, block, g, target):
        piece = held.at[block, pl.ds(g * per, per)]
        return pltpu.make_async_remote_copy(
            src_ref=piece, dst_ref=piece,
            send_sem=send_sem.at[way, step, g], recv_sem=recv_sem.at[block, g],
            device_id={"recv": target}, device_id_type=MESH,
        )

    def hand_part(way, step, block, target):
        piece = held.at[block, pl.ds(mixed * per, per - extra)]
        return pltpu.make_async_remote_copy(
            src_ref=piece, dst_ref=piece,
            send_sem=send_sem.at[way, step, mixed], recv_sem=recv_sem.at[block, mixed],
            device_id={"recv": target}, device_id_type=MESH,
        )

    def hand_rest(way, block, target):
        piece = held.at[block, mixed * per, :, pl.ds(cols, depth - cols)]
        return pltpu.make_async_remote_copy(
            src_ref=piece, dst_ref=piece,
            send_sem=send_sem.at[way, 0, mixed], recv_sem=recv_sem.at[block, mixed],
            device_id={"recv": target}, device_id_type=MESH,
        )

    def hand_last(way, block, n, target):
        piece = held.at[block, pl.ds((groups - 1) * per + n, 1)]
        return pltpu.make_async_remote_copy(
            src_ref=piece, dst_ref=piece,
            send_sem=fine_send.at[way, n], recv_sem=fine_recv.at[way, n],
            device_id={"recv": target}, device_id_type=MESH,
        )

    def pass_on(way, step, block, g, target, act):
        to_end = (me == line - 2) if way == 0 else (me == 1)
        last = to_end & (step == line - 2) & (g == groups - 1)
        part = to_end & (g == mixed) if extra else False
        plain = jnp.logical_not(last | part | (to_end & (g >= gone) & (g < groups - 1)))

        @pl.when(plain)
        def _():
            act(hand_on(way, step, block, g, target))

        @pl.when(last)
        def _():
            for n in range(per):
                act(hand_last(way, block, n, target))

        if extra:
            @pl.when(part & ((step > 0) | (cols == 0)))
            def _():
                act(hand_part(way, step, block, target))

            if cols:
                @pl.when(part & (step == 0))
                def _():
                    act(hand_rest(way, block, target))

    def lend(k, target):
        columns = pl.ds(pl.multiple_of(skipped * depth, LANES), (line - 1) * depth)
        return pltpu.make_async_remote_copy(
            src_ref=resp.at[:, first_lent + k, :, columns], dst_ref=guest.at[k],
            send_sem=guest_send.at[k], recv_sem=guest_recv.at[k],
            device_id={"recv": target}, device_id_type=MESH,
        )

    def lend_morsel(host, target):
        columns = pl.ds(pl.multiple_of(host * depth, LANES), cols)
        return pltpu.make_async_remote_copy(
            src_ref=resp.at[:, mixed * per, :, columns], dst_ref=morsel,
            send_sem=guest_send.at[lent + line - 2], recv_sem=guest_recv.at[lent + line - 2],
            device_id={"recv": target}, device_id_type=MESH,
        )

    def lend_last(n, target):
        columns = pl.ds(pl.multiple_of((n + skipped) * depth, LANES), depth)
        return pltpu.make_async_remote_copy(
            src_ref=resp.at[:, (groups - 1) * per - 1, :, columns],
            dst_ref=guest.at[lent - 1, :, :, pl.ds(n * depth, depth)],
            send_sem=guest_send.at[lent - 1 + n], recv_sem=guest_recv.at[lent - 1 + n],
            device_id={"recv": target}, device_id_type=MESH,
        )

    def give_back(place):
        copies = []
        for other in range(across):
            copies.append(pltpu.make_async_remote_copy(
                src_ref=back_out.at[other], dst_ref=back_in.at[mine],
                send_sem=back_send.at[other], recv_sem=back_recv.at[mine],
                device_id={"recv": place, "freq": other}, device_id_type=MESH,
            ))
        return copies

    def take_back(place):
        copies = []
        for other in range(across):
            copies.append(pltpu.make_async_remote_copy(
                src_ref=back_out.at[other], dst_ref=back_in.at[other],
                send_sem=back_send.at[other], recv_sem=back_recv.at[other],
                device_id={"recv": place, "freq": other}, device_id_type=MESH,
            ))
        return copies

    @pl.loop(0, groups)
    def _(g):
        @pl.when(has_right)
        def _():
            pass_on(0, 0, me, g, right, lambda copy: copy.start())

        @pl.when(has_left)
        def _():
            pass_on(1, 0, me, g, left, lambda copy: copy.start())

        @pl.when(g + 2 < groups)
        def _():
            convert(g + 2)

    def multiply(lhs, rhs):
        return lax.dot_general(
            lhs.reshape(2 * rows, lhs.shape[-1]), rhs, (((1,), (1,)), ((), ())),
            preferred_element_type=jnp.float32,
        )

    def of_block(block, g, count=per):
        columns = pl.ds(pl.multiple_of(block * depth, LANES), depth)
        parts = []
        for k in range(count):
            parts.append(multiply(resp[:, g * per + k, :, columns], held[block, g * per + k]))
        parts += [jnp.zeros((2 * rows, 2 * focal), jnp.float32)] * (per - count)
        return jnp.concatenate(parts, axis=1)

    @pl.loop(0, groups)
    def _(g):
        load_resp(g).wait()

    if lent:
        @pl.when(is_end)
        def _():
            if cols:
                lend_morsel(beside_end, beside_end).start()
            for k in range(lent - 1):
                lend(k, beside_end).start()
            for n in range(line - 1):
                lend_last(n, beside_end).start()

    @pl.loop(0, groups)
    def _(g):
        acc[g] = of_block(me, g)

    half = lax.rem(lax.broadcasted_iota(jnp.int32, (rows, LANES), 1), 2 * focal) < focal

    def combine(tile):
        real, imag = tile[:rows], tile[rows:]
        return real + jnp.where(
            half, -pltpu.roll(imag, LANES - focal, axis=1), pltpu.roll(imag, focal, axis=1)
        )

    def serve(slot):
        parts = []
        for n in range(per):
            k = lent - (slots - slot) * per + n
            if k == -1 and cols:
                lend_morsel(me, end).wait_recv()
                parts.append(multiply(morsel[...], held[me, mixed * per, :, :cols]))
                continue
            if k < 0:
                parts.append(jnp.zeros((2 * rows, 2 * focal), jnp.float32))
                continue
            if k < lent - 1:
                lend(k, end).wait_recv()
            total = None
            for n in range(line - 1):
                if k == lent - 1:
                    lend_last(n, end).wait_recv()
                term = multiply(guest[k, :, :, n * depth:(n + 1) * depth], held[n + skipped, first_lent + k])
                total = term if total is None else total + term
            parts.append(total)
        return combine(jnp.concatenate(parts, axis=1))

    def split_rows(tile, at, target):
        for d in range(across):
            target[d, at * owned:(at + 1) * owned, :] = tile[d * owned:(d + 1) * owned]

    def visit(t):
        step, g = 1 + t // groups, t % groups
        from_left, from_right = me - step, me + step
        due_left, due_right = from_left >= 0, from_right < line
        if lent:
            wanted = jnp.logical_not(is_end) | (g < gone) | (g == groups - 1)
            due_left, due_right = due_left & wanted, due_right & wanted
        if extra:
            part = is_end & (g == mixed)
            due_left, due_right = due_left & jnp.logical_not(part), due_right & jnp.logical_not(part)

            @pl.when(part)
            def _():
                block = jnp.where(is_first, from_right, from_left)

                @pl.when((step > 1) | (cols == 0))
                def _():
                    hand_part(jnp.where(is_first, 1, 0), 0, block, beside_end).wait_recv()
                    acc[mixed] = acc[mixed] + of_block(block, mixed, per - extra)

                if cols:
                    @pl.when(step == 1)
                    def _():
                        hand_rest(jnp.where(is_first, 1, 0), block, beside_end).wait_recv()
                        columns = pl.ds(pl.multiple_of(block * depth + cols, LANES), depth - cols)
                        tile = multiply(resp[:, mixed * per, :, columns], held[block, mixed * per, :, cols:])
                        acc[mixed, :, :2 * focal] = acc[mixed, :, :2 * focal] + tile

        left_block, right_block = jnp.maximum(from_left, 0), jnp.minimum(from_right, line - 1)

        @pl.when(due_left)
        def _():
            hand_on(0, 0, left_block, g, left).wait_recv()

            @pl.when(has_right & (step < line - 1))
            def _():
                pass_on(0, step, left_block, g, right, lambda copy: copy.start())

        @pl.when(due_right)
        def _():
            hand_on(1, 0, right_block, g, right).wait_recv()

            @pl.when(has_left & (step < line - 1))
            def _():
                pass_on(1, step, right_block, g, left, lambda copy: copy.start())

        @pl.loop(0, 2)
        def _(side):
            @pl.when(((side == 0) & due_left) | ((side == 1) & due_right))
            def _():
                acc[g] = acc[g] + of_block(jnp.where(side == 0, left_block, right_block), g)

        if slots > 1:
            @pl.when(is_host & (step == line - 2) & (g == groups - 2))
            def _():
                for slot in range(slots - 1):
                    split_rows(serve(slot), slot, back_out)

    def visit_end():
        @pl.when(is_end)
        def _():
            block = jnp.where(is_first, line - 1, 0)
            columns = pl.ds(pl.multiple_of(block * depth, LANES), depth)
            parts = []
            for n in range(per):
                hand_last(jnp.where(is_first, 1, 0), block, n, beside_end).wait_recv()
                k = (groups - 1) * per + n
                parts.append(multiply(resp[:, k, :, columns], held[block, k]))
            acc[groups - 1] = acc[groups - 1] + jnp.concatenate(parts, axis=1)

    @pl.loop(0, (line - 1) * groups - 1)
    def _(t):
        visit(t)

    def exchange(part, source, target):
        copies = []
        for hop in range(1, across):
            other = lax.rem(mine + hop, across)
            copies.append(pltpu.make_async_remote_copy(
                src_ref=source.at[other], dst_ref=target.at[mine],
                send_sem=x_send.at[part, hop], recv_sem=x_recv.at[part, hop],
                device_id={"freq": other}, device_id_type=MESH,
            ))
        copies.append(pltpu.make_async_copy(source.at[mine], target.at[mine], x_local.at[part]))
        return copies

    def lines(source, r, g):
        return source[:, g * owned + r, :]

    def transform(pieces, place):
        parts = []
        for source, count in pieces:
            for g in range(count):
                rows_of = [lines(source, r, g) for r in range(owned)]
                for m in range(2 * per):
                    lanes = [row[:, m * focal:(m + 1) * focal] for row in rows_of]
                    parts.append(jnp.concatenate(lanes, axis=1))
        values = jnp.concatenate(parts, axis=0)
        high = values.astype(jnp.bfloat16)
        low = (values - high.astype(jnp.float32)).astype(jnp.bfloat16)
        first = place * 2 * per * across
        span = slice(first, first + values.shape[0])

        def dot(a, b):
            return lax.dot_general(a, b, (((0,), (0,)), ((), ())), preferred_element_type=jnp.float32)

        return dot(high, table[0, span]) + (dot(low, table[0, span]) + dot(high, table[1, span]))

    for g in range(groups - 1):
        split_rows(combine(acc[g]), g, early_out)
    early = exchange(0, early_out, early_in)
    for copy in early:
        copy.start()
    if slots:
        @pl.when(jnp.logical_not(is_end))
        def _():
            back_in[...] = jnp.zeros_like(back_in)

    load_table.wait()
    load_onset.wait()
    load_finale.wait()
    for copy in early:
        copy.wait()
    traces[...] = transform([(early_in, groups - 1)], 0)
    visit_end()

    split_rows(combine(acc[groups - 1]), 0, late_out)
    late = exchange(1, late_out, late_in)
    for copy in late:
        copy.start()

    if slots:
        @pl.when(is_host)
        def _():
            split_rows(serve(slots - 1), slots - 1, back_out)
            for copy in give_back(end):
                copy.start()

    @pl.loop(0, (line - 1) * groups)
    def _(t):
        step, g = t // groups, t % groups

        @pl.when(has_right & (me - step >= 0))
        def _():
            pass_on(0, step, me, g, right, lambda copy: copy.wait_send())

        @pl.when(has_left & (me + step < line))
        def _():
            pass_on(1, step, me, g, left, lambda copy: copy.wait_send())

    if slots:
        @pl.when(is_end)
        def _():
            if cols:
                lend_morsel(beside_end, beside_end).wait_send()
            for k in range(lent - 1):
                lend(k, beside_end).wait_send()
            for n in range(line - 1):
                lend_last(n, beside_end).wait_send()

        @pl.when(is_host)
        def _():
            for copy in give_back(end):
                copy.wait_send()

    samples = lax.broadcasted_iota(jnp.int32, (focal, NT), 1)
    starts, ends = jnp.transpose(onset[...]), jnp.transpose(finale[...])
    for copy in late:
        copy.wait()
    late_pieces = [(late_in, 1)]
    if slots:
        late_pieces = [(back_in, slots)] + late_pieces

        @pl.when(is_end)
        def _():
            for copy in take_back(beside_end):
                copy.wait_recv()

    total = traces[...] + transform(late_pieces, groups - 1 - slots)
    for r in range(owned):
        inside = (samples >= starts[:, r:r + 1]) & (samples < ends[:, r:r + 1])
        windowed = jnp.where(inside, total[r * focal:(r + 1) * focal], 0.0)
        out_ref[:, r, :] = windowed


def per_device(line, across, response, focusing, window_onset, window_end):
    _, freqs, rows, sources = response.shape
    focal, depth = focusing.shape[2], focusing.shape[3]
    per = LANES // (2 * focal)
    groups = freqs // per
    owned = rows // across
    lent = lent_freqs(line, freqs, rows, focal, per)
    cols = lent_sources(line, freqs, rows, focal, per, lent, depth)
    slots = -(-lent // per)
    early_lines, late_lines, back_lines = (-(-count * owned // 8) * 8 for count in (groups - 1, 1, max(slots, 1)))
    tables = make_tables(across, groups, per)
    dma = pltpu.SemaphoreType.DMA
    return pl.pallas_call(
        functools.partial(spectra_kernel, line, across, lent, cols),
        out_shape=pltpu.VMEM((focal, owned, NT), jnp.float32),
        in_specs=[pl.BlockSpec(memory_space=pl.ANY)] * 5,
        out_specs=pl.BlockSpec(memory_space=pltpu.VMEM),
        scratch_shapes=[
            pltpu.VMEM(response.shape, jnp.bfloat16),
            pltpu.VMEM(focusing.shape, jnp.float32),
            pltpu.VMEM((line, freqs, 2 * focal, depth), jnp.bfloat16),
            pltpu.VMEM((max(lent, 1), 2, rows, (line - 1) * depth), jnp.bfloat16),
            pltpu.VMEM((2, rows, max(cols, LANES)), jnp.bfloat16),
            pltpu.VMEM((groups, 2 * rows, LANES), jnp.float32),
            pltpu.VMEM((across, back_lines, LANES), jnp.float32),
            pltpu.VMEM((across, back_lines, LANES), jnp.float32),
            pltpu.VMEM(tables.shape, jnp.bfloat16),
            pltpu.VMEM((owned, focal), jnp.int32),
            pltpu.VMEM((owned, focal), jnp.int32),
            pltpu.VMEM((owned * focal, NT), jnp.float32),
            pltpu.VMEM((across, early_lines, LANES), jnp.float32),
            pltpu.VMEM((across, early_lines, LANES), jnp.float32),
            pltpu.VMEM((across, late_lines, LANES), jnp.float32),
            pltpu.VMEM((across, late_lines, LANES), jnp.float32),
            dma((groups,)),
            dma((groups,)),
            dma,
            dma,
            dma,
            dma((2, max(line - 1, 1), groups)),
            dma((line, groups)),
            dma((2, per)),
            dma((2, per)),
            dma((lent + line,)),
            dma((lent + line,)),
            dma((across,)),
            dma((across,)),
            dma((2, across)),
            dma((2, across)),
            dma((2,)),
        ],
        compiler_params=pltpu.CompilerParams(
            collective_id=0, has_side_effects=True, vmem_limit_bytes=60000 * 1024
        ),
    )(response, focusing, tables, window_onset.T, window_end.T)


def solution(mesh):
    line, across = mesh.shape["recv"], mesh.shape["freq"]
    in_specs = (
        P(None, "freq", "recv", None),
        P(None, "freq", None, "recv"),
        P(None, ("recv", "freq")),
        P(None, ("recv", "freq")),
    )
    out_specs = P(None, ("recv", "freq"), None)
    return jax.shard_map(
        functools.partial(per_device, line, across),
        mesh=mesh, in_specs=in_specs, out_specs=out_specs, check_vma=False,
    )
```

```python
import functools
import math

import jax
import jax.numpy as jnp
import numpy as np
from jax import lax
from jax.experimental import pallas as pl
from jax.experimental.pallas import tpu as pltpu
from jax.sharding import PartitionSpec as P

NT = 1024
LANES = 128
MESH = pl.DeviceIdType.MESH


def make_tables(across, groups, per):
    freqs = groups * per
    count = across * freqs
    phase = (np.arange(count)[:, None] * np.arange(NT)[None, :] % NT) * (2.0 * math.pi / NT)
    scale = 1.0 / math.sqrt(count)
    table = np.stack([np.cos(phase) * scale, -np.sin(phase) * scale], 1)
    table = table.reshape(across, groups, per, 2, NT).transpose(1, 2, 3, 0, 4).reshape(-1, NT)
    high = table.astype(np.float32).astype(jnp.bfloat16)
    low = (table - high.astype(np.float64)).astype(np.float32).astype(jnp.bfloat16)
    return np.stack([high, low])


def lent_freqs(line, freqs, rows, focal, per):
    if line < 4:
        return 0
    even = (line - 2) * freqs * focal // ((line - 1) * (focal + rows))
    return max(min(even, freqs - per), 0)


def lent_sources(line, freqs, rows, focal, per, lent, depth):
    if lent % per != per - 1:
        return 0
    even = (line - 2) * freqs * focal * depth // (focal + rows) - (line - 1) * lent * depth
    return min(-(-even // LANES) * LANES, depth - LANES)


def spectra_kernel(
    line, across, lent, cols, resp_hbm, focus_hbm, table_hbm, onset_hbm, end_hbm, out_ref,
    resp, focus, held, guest, morsel, acc, back_out, back_in, table, onset, finale, traces,
    early_out, early_in, late_out, late_in,
    resp_sem, focus_sem, table_sem, onset_sem, finale_sem, send_sem, part_sem, recv_sem, fine_send, fine_recv,
    guest_send, morsel_send, guest_recv, back_send, back_recv, x_send, x_recv,
):
    me = lax.axis_index("recv")
    mine = lax.axis_index("freq")
    _, freqs, rows, _ = resp_hbm.shape
    focal, depth = focus_hbm.shape[2], focus_hbm.shape[3]
    groups = acc.shape[0]
    per = freqs // groups
    owned = rows // across
    slots = -(-lent // per)
    mixed = groups - 1 - slots
    extra = lent % per
    gone = mixed + 1 if extra else mixed
    first_lent = (groups - 1) * per - lent
    rear = max(min(lent, per) - 1, 0)
    parts_lent = [(0, max(lent - 1 - rear, 0)), (max(lent - 1 - rear, 0), rear)]
    has_left, has_right = me > 0, me < line - 1
    is_first, is_last = me == 0, me == line - 1
    left, right = jnp.maximum(me - 1, 0), jnp.minimum(me + 1, line - 1)
    is_end = is_first | is_last
    is_host = (me == 1) | (me == line - 2)
    beside_end = jnp.where(is_first, right, left)
    end = jnp.where(me == 1, 0, line - 1)
    skipped = jnp.where(is_first | (me == 1), 1, 0)

    leads = min(2, groups - 1)

    def load_focus(g):
        count = per if g < leads else (groups - leads) * per
        return pltpu.make_async_copy(
            focus_hbm.at[:, pl.ds(g * per, count)], focus.at[:, pl.ds(g * per, count)], focus_sem.at[g]
        )

    load_resp = pltpu.make_async_copy(resp_hbm, resp, resp_sem)

    for g in range(leads + 1):
        load_focus(g).start()

    barrier = pltpu.get_barrier_semaphore()

    @pl.when(has_left)
    def _():
        pl.semaphore_signal(barrier, inc=1, device_id={"recv": left}, device_id_type=MESH)

    @pl.when(has_right)
    def _():
        pl.semaphore_signal(barrier, inc=1, device_id={"recv": right}, device_id_type=MESH)

    for hop in range(1, across):
        other = lax.rem(mine + hop, across)
        pl.semaphore_signal(barrier, inc=1, device_id={"freq": other}, device_id_type=MESH)

    load_resp.start()

    load_table = pltpu.make_async_copy(table_hbm, table, table_sem)
    load_table.start()
    load_onset = pltpu.make_async_copy(onset_hbm, onset, onset_sem)
    load_onset.start()
    load_finale = pltpu.make_async_copy(end_hbm, finale, finale_sem)
    load_finale.start()

    def convert(g):
        for i in range(per):
            k = g * per + i
            for part in range(2):
                held[me, k, part * focal:(part + 1) * focal, :] = focus[part, k].astype(jnp.bfloat16)

    for g in range(leads):
        load_focus(g).wait()
        convert(g)

    beside = has_left.astype(jnp.int32) + has_right.astype(jnp.int32)
    pl.semaphore_wait(barrier, across - 1 + beside)

    def hand_on(way, step, block, g, target):
        piece = held.at[block, pl.ds(g * per, per)]
        return pltpu.make_async_remote_copy(
            src_ref=piece, dst_ref=piece,
            send_sem=send_sem.at[way, step], recv_sem=recv_sem.at[block - way, g],
            device_id={"recv": target}, device_id_type=MESH,
        )

    def hand_part(way, step, block, target):
        piece = held.at[block, pl.ds(mixed * per, per - extra)]
        return pltpu.make_async_remote_copy(
            src_ref=piece, dst_ref=piece,
            send_sem=part_sem.at[step], recv_sem=recv_sem.at[block - way, mixed],
            device_id={"recv": target}, device_id_type=MESH,
        )

    def hand_rest(way, block, target):
        piece = held.at[block, mixed * per, :, pl.ds(cols, depth - cols)]
        return pltpu.make_async_remote_copy(
            src_ref=piece, dst_ref=piece,
            send_sem=part_sem.at[0], recv_sem=recv_sem.at[block - way, mixed],
            device_id={"recv": target}, device_id_type=MESH,
        )

    def hand_last(way, block, n, target):
        piece = held.at[block, pl.ds((groups - 1) * per + n, 1)]
        return pltpu.make_async_remote_copy(
            src_ref=piece, dst_ref=piece,
            send_sem=fine_send, recv_sem=fine_recv.at[n],
            device_id={"recv": target}, device_id_type=MESH,
        )

    def pass_on(way, step, block, g, target, act):
        to_end = (me == line - 2) if way == 0 else (me == 1)
        last = to_end & (step == line - 2) & (g == groups - 1)
        part = to_end & (g == mixed) if extra else False
        plain = jnp.logical_not(last | part | (to_end & (g >= gone) & (g < groups - 1)))

        @pl.when(plain)
        def _():
            act(hand_on(way, step, block, g, target))

        @pl.when(last)
        def _():
            for n in range(per):
                act(hand_last(way, block, n, target))

        if extra:
            @pl.when(part & ((step > 0) | (cols == 0)))
            def _():
                act(hand_part(way, step, block, target))

            if cols:
                @pl.when(part & (step == 0))
                def _():
                    act(hand_rest(way, block, target))

    def lend(part, target):
        first, count = parts_lent[part]
        columns = pl.ds(pl.multiple_of(skipped * depth, LANES), (line - 1) * depth)
        return pltpu.make_async_remote_copy(
            src_ref=resp.at[:, pl.ds(first_lent + first, count), :, columns],
            dst_ref=guest.at[:, pl.ds(first, count)],
            send_sem=guest_send, recv_sem=guest_recv.at[part],
            device_id={"recv": target}, device_id_type=MESH,
        )

    def lend_morsel(host, target):
        columns = pl.ds(pl.multiple_of(host * depth, LANES), cols)
        return pltpu.make_async_remote_copy(
            src_ref=resp.at[:, mixed * per, :, columns], dst_ref=morsel,
            send_sem=morsel_send, recv_sem=guest_recv.at[2],
            device_id={"recv": target}, device_id_type=MESH,
        )

    def lend_last(n, target):
        columns = pl.ds(pl.multiple_of((n + skipped) * depth, LANES), depth)
        return pltpu.make_async_remote_copy(
            src_ref=resp.at[:, (groups - 1) * per - 1, :, columns],
            dst_ref=guest.at[:, lent - 1, :, pl.ds(n * depth, depth)],
            send_sem=guest_send, recv_sem=guest_recv.at[3 + n],
            device_id={"recv": target}, device_id_type=MESH,
        )

    def give_back(other, place):
        return pltpu.make_async_remote_copy(
            src_ref=back_out.at[other], dst_ref=back_in.at[mine], send_sem=back_send, recv_sem=back_recv,
            device_id={"recv": place, "freq": other}, device_id_type=MESH,
        )

    def all_back(place):
        return pltpu.make_async_remote_copy(
            src_ref=back_out, dst_ref=back_in, send_sem=back_send, recv_sem=back_recv,
            device_id={"recv": place}, device_id_type=MESH,
        )

    load_focus(leads).wait()

    @pl.loop(0, groups)
    def _(g):
        @pl.when(has_right)
        def _():
            pass_on(0, 0, me, g, right, lambda copy: copy.start())

        @pl.when(has_left)
        def _():
            pass_on(1, 0, me, g, left, lambda copy: copy.start())

        @pl.when(g + leads < groups)
        def _():
            convert(g + leads)

    def multiply(lhs, rhs):
        return lax.dot_general(
            lhs.reshape(2 * rows, lhs.shape[-1]), rhs, (((1,), (1,)), ((), ())),
            preferred_element_type=jnp.float32,
        )

    def of_block(block, g, count=per):
        columns = pl.ds(pl.multiple_of(block * depth, LANES), depth)
        parts = []
        for k in range(count):
            parts.append(multiply(resp[:, g * per + k, :, columns], held[block, g * per + k]))
        parts += [jnp.zeros((2 * rows, 2 * focal), jnp.float32)] * (per - count)
        return jnp.concatenate(parts, axis=1)

    load_resp.wait()

    if lent:
        @pl.when(is_end)
        def _():
            if cols:
                lend_morsel(beside_end, beside_end).start()
            for part in range(2):
                if parts_lent[part][1]:
                    lend(part, beside_end).start()
            for n in range(line - 1):
                lend_last(n, beside_end).start()

    @pl.loop(0, groups)
    def _(g):
        acc[g] = of_block(me, g)

    half = lax.rem(lax.broadcasted_iota(jnp.int32, (rows, LANES), 1), 2 * focal) < focal

    def combine(tile):
        real, imag = tile[:rows], tile[rows:]
        return real + jnp.where(
            half, -pltpu.roll(imag, LANES - focal, axis=1), pltpu.roll(imag, focal, axis=1)
        )

    def serve(slot):
        parts = []
        for n in range(per):
            k = lent - (slots - slot) * per + n
            if k == -1 and cols:
                lend_morsel(me, end).wait_recv()
                parts.append(multiply(morsel[...], held[me, mixed * per, :, :cols]))
                continue
            if k < 0:
                parts.append(jnp.zeros((2 * rows, 2 * focal), jnp.float32))
                continue
            for part in range(2):
                if parts_lent[part][1] and k == parts_lent[part][0]:
                    lend(part, end).wait_recv()
            total = None
            for n in range(line - 1):
                if k == lent - 1:
                    lend_last(n, end).wait_recv()
                term = multiply(guest[:, k, :, n * depth:(n + 1) * depth], held[n + skipped, first_lent + k])
                total = term if total is None else total + term
            parts.append(total)
        return combine(jnp.concatenate(parts, axis=1))

    def split_rows(tile, at, target):
        for d in range(across):
            target[d, at * owned:(at + 1) * owned, :] = tile[d * owned:(d + 1) * owned]

    def visit(t):
        step, g = 1 + t // groups, t % groups
        from_left, from_right = me - step, me + step
        due_left, due_right = from_left >= 0, from_right < line
        if lent:
            wanted = jnp.logical_not(is_end) | (g < gone) | (g == groups - 1)
            due_left, due_right = due_left & wanted, due_right & wanted
        if extra:
            part = is_end & (g == mixed)
            due_left, due_right = due_left & jnp.logical_not(part), due_right & jnp.logical_not(part)

            @pl.when(part)
            def _():
                block = jnp.where(is_first, from_right, from_left)

                @pl.when((step > 1) | (cols == 0))
                def _():
                    hand_part(jnp.where(is_first, 1, 0), 0, block, beside_end).wait_recv()
                    acc[mixed] = acc[mixed] + of_block(block, mixed, per - extra)

                if cols:
                    @pl.when(step == 1)
                    def _():
                        hand_rest(jnp.where(is_first, 1, 0), block, beside_end).wait_recv()
                        columns = pl.ds(pl.multiple_of(block * depth + cols, LANES), depth - cols)
                        tile = multiply(resp[:, mixed * per, :, columns], held[block, mixed * per, :, cols:])
                        acc[mixed, :, :2 * focal] = acc[mixed, :, :2 * focal] + tile

        left_block, right_block = jnp.maximum(from_left, 0), jnp.minimum(from_right, line - 1)

        @pl.when(due_left)
        def _():
            hand_on(0, 0, left_block, g, left).wait_recv()

            @pl.when(has_right & (step < line - 1))
            def _():
                pass_on(0, step, left_block, g, right, lambda copy: copy.start())

        @pl.when(due_right)
        def _():
            hand_on(1, 0, right_block, g, right).wait_recv()

            @pl.when(has_left & (step < line - 1))
            def _():
                pass_on(1, step, right_block, g, left, lambda copy: copy.start())

        @pl.loop(0, 2)
        def _(side):
            @pl.when(((side == 0) & due_left) | ((side == 1) & due_right))
            def _():
                acc[g] = acc[g] + of_block(jnp.where(side == 0, left_block, right_block), g)

        if slots > 1:
            @pl.when(is_host & (step == line - 2) & (g == groups - 2))
            def _():
                for slot in range(slots - 1):
                    split_rows(serve(slot), slot, back_out)

    def visit_end():
        @pl.when(is_end)
        def _():
            block = jnp.where(is_first, line - 1, 0)
            columns = pl.ds(pl.multiple_of(block * depth, LANES), depth)
            parts = []
            for n in range(per):
                hand_last(jnp.where(is_first, 1, 0), block, n, beside_end).wait_recv()
                k = (groups - 1) * per + n
                parts.append(multiply(resp[:, k, :, columns], held[block, k]))
            acc[groups - 1] = acc[groups - 1] + jnp.concatenate(parts, axis=1)

    @pl.loop(0, (line - 1) * groups - 1)
    def _(t):
        visit(t)

    def partners():
        hops = list(range(1, across))
        if across & (across - 1):
            return [lax.rem(mine + hop, across) for hop in hops]
        hops.sort(key=lambda hop: -bin(hop >> 1).count("1"))
        bits = [1 << n for n in range(across.bit_length() - 1)]
        return [mine + sum(b * (1 - 2 * (mine // b % 2)) for b in bits if hop & b) for hop in hops]

    def exchange(part, source, target):
        for other in partners():
            pltpu.make_async_remote_copy(
                src_ref=source.at[other], dst_ref=target.at[mine],
                send_sem=x_send.at[part], recv_sem=x_recv.at[part],
                device_id={"freq": other}, device_id_type=MESH,
            ).start()
        target[mine] = source[mine]

    def exchanged(part, source, target):
        pltpu.make_async_remote_copy(
            src_ref=source.at[pl.ds(0, across - 1)], dst_ref=target.at[pl.ds(0, across - 1)],
            send_sem=x_send.at[part], recv_sem=x_recv.at[part],
            device_id={"freq": lax.rem(mine + 1, across)}, device_id_type=MESH,
        ).wait()

    def lines(source, r, g):
        return source[:, g * owned + r, :]

    def transform(pieces, place):
        parts = []
        for source, count in pieces:
            for g in range(count):
                rows_of = [lines(source, r, g) for r in range(owned)]
                for m in range(2 * per):
                    lanes = [row[:, m * focal:(m + 1) * focal] for row in rows_of]
                    parts.append(jnp.concatenate(lanes, axis=1))
        values = jnp.concatenate(parts, axis=0)
        high = values.astype(jnp.bfloat16)
        low = (values - high.astype(jnp.float32)).astype(jnp.bfloat16)
        first = place * 2 * per * across
        span = slice(first, first + values.shape[0])

        def dot(a, b):
            return lax.dot_general(a, b, (((0,), (0,)), ((), ())), preferred_element_type=jnp.float32)

        return dot(high, table[0, span]) + (dot(low, table[0, span]) + dot(high, table[1, span]))

    for g in range(groups - 1):
        split_rows(combine(acc[g]), g, early_out)
    exchange(0, early_out, early_in)
    if slots:
        @pl.when(jnp.logical_not(is_end))
        def _():
            back_in[...] = jnp.zeros_like(back_in)

    load_table.wait()
    load_onset.wait()
    load_finale.wait()
    exchanged(0, early_out, early_in)
    traces[...] = transform([(early_in, groups - 1)], 0)
    visit_end()

    split_rows(combine(acc[groups - 1]), 0, late_out)
    exchange(1, late_out, late_in)

    if slots:
        @pl.when(is_host)
        def _():
            split_rows(serve(slots - 1), slots - 1, back_out)
            for other in range(across):
                give_back(other, end).start()

    def drained(way, step, target):
        to_end = (me == line - 2) if way == 0 else (me == 1)

        def pieces(count):
            piece = held.at[me, pl.ds(0, count)]
            return pltpu.make_async_remote_copy(
                src_ref=piece, dst_ref=piece, send_sem=send_sem.at[way, step], recv_sem=recv_sem.at[0, 0],
                device_id={"recv": target}, device_id_type=MESH,
            )

        @pl.when(jnp.logical_not(to_end))
        def _():
            pieces(freqs).wait_send()

        @pl.when(to_end)
        def _():
            count = mixed * per if step == line - 2 else (mixed + 1) * per
            if count:
                pieces(count).wait_send()
            if extra and (step or not cols):
                hand_part(way, step, me, target).wait_send()
            if extra and cols and step == 0:
                hand_rest(way, me, target).wait_send()
            if step == line - 2:
                piece = held.at[me, pl.ds(0, per)]
                pltpu.make_async_remote_copy(
                    src_ref=piece, dst_ref=piece, send_sem=fine_send, recv_sem=fine_recv.at[0],
                    device_id={"recv": target}, device_id_type=MESH,
                ).wait_send()

    for step in range(line - 1):
        @pl.when(has_right & (me - step >= 0))
        def _():
            drained(0, step, right)

        @pl.when(has_left & (me + step < line))
        def _():
            drained(1, step, left)

    if slots:
        @pl.when(is_end)
        def _():
            pltpu.make_async_remote_copy(
                src_ref=guest, dst_ref=guest, send_sem=guest_send, recv_sem=guest_recv.at[0],
                device_id={"recv": beside_end}, device_id_type=MESH,
            ).wait_send()
            if cols:
                lend_morsel(beside_end, beside_end).wait_send()

        @pl.when(is_host)
        def _():
            all_back(end).wait_send()

    samples = lax.broadcasted_iota(jnp.int32, (focal, NT), 1)
    starts, ends = jnp.transpose(onset[...]), jnp.transpose(finale[...])
    exchanged(1, late_out, late_in)
    late_pieces = [(late_in, 1)]
    if slots:
        late_pieces = [(back_in, slots)] + late_pieces

        @pl.when(is_end)
        def _():
            all_back(beside_end).wait_recv()

    total = traces[...] + transform(late_pieces, groups - 1 - slots)
    for r in range(owned):
        inside = (samples >= starts[:, r:r + 1]) & (samples < ends[:, r:r + 1])
        windowed = jnp.where(inside, total[r * focal:(r + 1) * focal], 0.0)
        out_ref[:, r, :] = windowed


def per_device(line, across, response, focusing, window_onset, window_end):
    _, freqs, rows, sources = response.shape
    focal, depth = focusing.shape[2], focusing.shape[3]
    per = LANES // (2 * focal)
    groups = freqs // per
    owned = rows // across
    lent = lent_freqs(line, freqs, rows, focal, per)
    cols = lent_sources(line, freqs, rows, focal, per, lent, depth)
    slots = -(-lent // per)
    early_lines, late_lines, back_lines = (-(-count * owned // 8) * 8 for count in (groups - 1, 1, max(slots, 1)))
    tables = make_tables(across, groups, per)
    dma = pltpu.SemaphoreType.DMA
    return pl.pallas_call(
        functools.partial(spectra_kernel, line, across, lent, cols),
        out_shape=pltpu.VMEM((focal, owned, NT), jnp.float32),
        in_specs=[pl.BlockSpec(memory_space=pl.ANY)] * 5,
        out_specs=pl.BlockSpec(memory_space=pltpu.VMEM),
        scratch_shapes=[
            pltpu.VMEM(response.shape, jnp.bfloat16),
            pltpu.VMEM(focusing.shape, jnp.float32),
            pltpu.VMEM((line, freqs, 2 * focal, depth), jnp.bfloat16),
            pltpu.VMEM((2, max(lent, 1), rows, (line - 1) * depth), jnp.bfloat16),
            pltpu.VMEM((2, rows, max(cols, LANES)), jnp.bfloat16),
            pltpu.VMEM((groups, 2 * rows, LANES), jnp.float32),
            pltpu.VMEM((across, back_lines, LANES), jnp.float32),
            pltpu.VMEM((across, back_lines, LANES), jnp.float32),
            pltpu.VMEM(tables.shape, jnp.bfloat16),
            pltpu.VMEM((owned, focal), jnp.int32),
            pltpu.VMEM((owned, focal), jnp.int32),
            pltpu.VMEM((owned * focal, NT), jnp.float32),
            pltpu.VMEM((across, early_lines, LANES), jnp.float32),
            pltpu.VMEM((across, early_lines, LANES), jnp.float32),
            pltpu.VMEM((across, late_lines, LANES), jnp.float32),
            pltpu.VMEM((across, late_lines, LANES), jnp.float32),
            dma,
            dma((min(2, groups - 1) + 1,)),
            dma,
            dma,
            dma,
            dma((2, max(line - 1, 1))),
            dma((max(line - 1, 1),)),
            dma((max(line - 1, 1), groups)),
            dma,
            dma((per,)),
            dma,
            dma,
            dma((line + 2,)),
            dma,
            dma,
            dma((2,)),
            dma((2,)),
        ],
        compiler_params=pltpu.CompilerParams(
            collective_id=0, has_side_effects=True, vmem_limit_bytes=60000 * 1024
        ),
    )(response, focusing, tables, window_onset.T, window_end.T)


def solution(mesh):
    line, across = mesh.shape["recv"], mesh.shape["freq"]
    in_specs = (
        P(None, "freq", "recv", None),
        P(None, "freq", None, "recv"),
        P(None, ("recv", "freq")),
        P(None, ("recv", "freq")),
    )
    out_specs = P(None, ("recv", "freq"), None)
    return jax.shard_map(
        functools.partial(per_device, line, across),
        mesh=mesh, in_specs=in_specs, out_specs=out_specs, check_vma=False,
    )
```

```python
import functools
import math

import jax
import jax.numpy as jnp
import numpy as np
from jax import lax
from jax.experimental import pallas as pl
from jax.experimental.pallas import tpu as pltpu
from jax.sharding import PartitionSpec as P

NT = 1024
LANES = 128
MESH = pl.DeviceIdType.MESH


def make_tables(across, groups, per):
    freqs = groups * per
    count = across * freqs
    phase = (np.arange(count)[:, None] * np.arange(NT)[None, :] % NT) * (2.0 * math.pi / NT)
    scale = 1.0 / math.sqrt(count)
    table = np.stack([np.cos(phase) * scale, -np.sin(phase) * scale], 1)
    table = table.reshape(across, groups, per, 2, NT).transpose(1, 2, 3, 0, 4).reshape(-1, NT)
    high = table.astype(np.float32).astype(jnp.bfloat16)
    low = (table - high.astype(np.float64)).astype(np.float32).astype(jnp.bfloat16)
    return np.stack([high, low])


def lent_freqs(line, freqs, rows, focal, per):
    if line < 4:
        return 0
    even = (line - 2) * freqs * focal // ((line - 1) * (focal + rows))
    return max(min(even, freqs - per), 0)


def lent_sources(line, freqs, rows, focal, per, lent, depth):
    if lent % per != per - 1:
        return 0
    even = (line - 2) * freqs * focal * depth // (focal + rows) - (line - 1) * lent * depth
    return min(even // LANES * LANES, depth - LANES)


def spectra_kernel(
    line, across, lent, cols, resp_hbm, focus_hbm, table_hbm, onset_hbm, end_hbm, out_ref,
    resp, focus, held, guest, morsel, acc, back_out, back_in, table, onset, finale, traces,
    early_out, early_in, late_out, late_in,
    resp_sem, focus_sem, table_sem, onset_sem, finale_sem, send_sem, part_sem, recv_sem, fine_send, fine_recv,
    guest_send, morsel_send, guest_recv, back_send, back_recv, x_send, x_recv,
):
    me = lax.axis_index("recv")
    mine = lax.axis_index("freq")
    _, freqs, rows, _ = resp_hbm.shape
    focal, depth = focus_hbm.shape[2], focus_hbm.shape[3]
    groups = acc.shape[0]
    per = freqs // groups
    owned = rows // across
    slots = -(-lent // per)
    mixed = groups - 1 - slots
    extra = lent % per
    gone = mixed + 1 if extra else mixed
    first_lent = (groups - 1) * per - lent
    rear = max(min(lent, per) - 1, 0)
    parts_lent = [(0, max(lent - 1 - rear, 0)), (max(lent - 1 - rear, 0), rear)]
    has_left, has_right = me > 0, me < line - 1
    is_first, is_last = me == 0, me == line - 1
    left, right = jnp.maximum(me - 1, 0), jnp.minimum(me + 1, line - 1)
    is_end = is_first | is_last
    is_host = (me == 1) | (me == line - 2)
    beside_end = jnp.where(is_first, right, left)
    end = jnp.where(me == 1, 0, line - 1)
    skipped = jnp.where(is_first | (me == 1), 1, 0)

    leads = min(2, groups - 1)

    def load_focus(g):
        count = per if g < leads else (groups - leads) * per
        return pltpu.make_async_copy(
            focus_hbm.at[:, pl.ds(g * per, count)], focus.at[:, pl.ds(g * per, count)], focus_sem.at[g]
        )

    load_resp = pltpu.make_async_copy(resp_hbm, resp, resp_sem)

    for g in range(leads + 1):
        load_focus(g).start()

    barrier = pltpu.get_barrier_semaphore()

    @pl.when(has_left)
    def _():
        pl.semaphore_signal(barrier, inc=1, device_id={"recv": left}, device_id_type=MESH)

    @pl.when(has_right)
    def _():
        pl.semaphore_signal(barrier, inc=1, device_id={"recv": right}, device_id_type=MESH)

    for hop in range(1, across):
        other = lax.rem(mine + hop, across)
        pl.semaphore_signal(barrier, inc=1, device_id={"freq": other}, device_id_type=MESH)

    load_resp.start()

    load_table = pltpu.make_async_copy(table_hbm, table, table_sem)
    load_table.start()
    load_onset = pltpu.make_async_copy(onset_hbm, onset, onset_sem)
    load_onset.start()
    load_finale = pltpu.make_async_copy(end_hbm, finale, finale_sem)
    load_finale.start()

    def convert(g):
        for i in range(per):
            k = g * per + i
            for part in range(2):
                held[me, k, part * focal:(part + 1) * focal, :] = focus[part, k].astype(jnp.bfloat16)

    for g in range(leads):
        load_focus(g).wait()
        convert(g)

    beside = has_left.astype(jnp.int32) + has_right.astype(jnp.int32)
    pl.semaphore_wait(barrier, across - 1 + beside)

    def hand_on(way, step, block, g, target):
        piece = held.at[block, pl.ds(g * per, per)]
        return pltpu.make_async_remote_copy(
            src_ref=piece, dst_ref=piece,
            send_sem=send_sem.at[way, step], recv_sem=recv_sem.at[block - way, g],
            device_id={"recv": target}, device_id_type=MESH,
        )

    def hand_part(way, step, block, target):
        piece = held.at[block, pl.ds(mixed * per, per - extra)]
        return pltpu.make_async_remote_copy(
            src_ref=piece, dst_ref=piece,
            send_sem=part_sem.at[step], recv_sem=recv_sem.at[block - way, mixed],
            device_id={"recv": target}, device_id_type=MESH,
        )

    def hand_rest(way, block, target):
        piece = held.at[block, mixed * per, :, pl.ds(cols, depth - cols)]
        return pltpu.make_async_remote_copy(
            src_ref=piece, dst_ref=piece,
            send_sem=part_sem.at[0], recv_sem=recv_sem.at[block - way, mixed],
            device_id={"recv": target}, device_id_type=MESH,
        )

    def hand_last(way, block, n, target):
        piece = held.at[block, pl.ds((groups - 1) * per + n, 1)]
        return pltpu.make_async_remote_copy(
            src_ref=piece, dst_ref=piece,
            send_sem=fine_send, recv_sem=fine_recv.at[n],
            device_id={"recv": target}, device_id_type=MESH,
        )

    def pass_on(way, step, block, g, target, act):
        to_end = (me == line - 2) if way == 0 else (me == 1)
        last = to_end & (step == line - 2) & (g == groups - 1)
        part = to_end & (g == mixed) if extra else False
        plain = jnp.logical_not(last | part | (to_end & (g >= gone) & (g < groups - 1)))

        @pl.when(plain)
        def _():
            act(hand_on(way, step, block, g, target))

        @pl.when(last)
        def _():
            for n in range(per):
                act(hand_last(way, block, n, target))

        if extra:
            @pl.when(part & ((step > 0) | (cols == 0)))
            def _():
                act(hand_part(way, step, block, target))

            if cols:
                @pl.when(part & (step == 0))
                def _():
                    act(hand_rest(way, block, target))

    def lend(part, target):
        first, count = parts_lent[part]
        columns = pl.ds(pl.multiple_of(skipped * depth, LANES), (line - 1) * depth)
        return pltpu.make_async_remote_copy(
            src_ref=resp.at[:, pl.ds(first_lent + first, count), :, columns],
            dst_ref=guest.at[:, pl.ds(first, count)],
            send_sem=guest_send, recv_sem=guest_recv.at[part],
            device_id={"recv": target}, device_id_type=MESH,
        )

    def lend_morsel(host, target):
        columns = pl.ds(pl.multiple_of(host * depth, LANES), cols)
        return pltpu.make_async_remote_copy(
            src_ref=resp.at[:, mixed * per, :, columns], dst_ref=morsel,
            send_sem=morsel_send, recv_sem=guest_recv.at[2],
            device_id={"recv": target}, device_id_type=MESH,
        )

    def lend_last(n, target):
        columns = pl.ds(pl.multiple_of((n + skipped) * depth, LANES), depth)
        return pltpu.make_async_remote_copy(
            src_ref=resp.at[:, (groups - 1) * per - 1, :, columns],
            dst_ref=guest.at[:, lent - 1, :, pl.ds(n * depth, depth)],
            send_sem=guest_send, recv_sem=guest_recv.at[3 + n],
            device_id={"recv": target}, device_id_type=MESH,
        )

    def give_back(other, place):
        return pltpu.make_async_remote_copy(
            src_ref=back_out.at[other], dst_ref=back_in.at[mine], send_sem=back_send, recv_sem=back_recv,
            device_id={"recv": place, "freq": other}, device_id_type=MESH,
        )

    def all_back(place):
        return pltpu.make_async_remote_copy(
            src_ref=back_out, dst_ref=back_in, send_sem=back_send, recv_sem=back_recv,
            device_id={"recv": place}, device_id_type=MESH,
        )

    load_focus(leads).wait()

    @pl.loop(0, groups)
    def _(g):
        @pl.when(has_right)
        def _():
            pass_on(0, 0, me, g, right, lambda copy: copy.start())

        @pl.when(has_left)
        def _():
            pass_on(1, 0, me, g, left, lambda copy: copy.start())

        @pl.when(g + leads < groups)
        def _():
            convert(g + leads)

    def multiply(lhs, rhs):
        return lax.dot_general(
            lhs.reshape(2 * rows, lhs.shape[-1]), rhs, (((1,), (1,)), ((), ())),
            preferred_element_type=jnp.float32,
        )

    def of_block(block, g, count=per):
        columns = pl.ds(pl.multiple_of(block * depth, LANES), depth)
        parts = []
        for k in range(count):
            parts.append(multiply(resp[:, g * per + k, :, columns], held[block, g * per + k]))
        parts += [jnp.zeros((2 * rows, 2 * focal), jnp.float32)] * (per - count)
        return jnp.concatenate(parts, axis=1)

    load_resp.wait()

    if lent:
        @pl.when(is_end)
        def _():
            if cols:
                lend_morsel(beside_end, beside_end).start()
            for part in range(2):
                if parts_lent[part][1]:
                    lend(part, beside_end).start()
            for n in range(line - 1):
                lend_last(n, beside_end).start()

    @pl.loop(0, groups)
    def _(g):
        acc[g] = of_block(me, g)

    half = lax.rem(lax.broadcasted_iota(jnp.int32, (rows, LANES), 1), 2 * focal) < focal

    def combine(tile):
        real, imag = tile[:rows], tile[rows:]
        return real + jnp.where(
            half, -pltpu.roll(imag, LANES - focal, axis=1), pltpu.roll(imag, focal, axis=1)
        )

    def serve(slot):
        parts = []
        for n in range(per):
            k = lent - (slots - slot) * per + n
            if k == -1 and cols:
                lend_morsel(me, end).wait_recv()
                parts.append(multiply(morsel[...], held[me, mixed * per, :, :cols]))
                continue
            if k < 0:
                parts.append(jnp.zeros((2 * rows, 2 * focal), jnp.float32))
                continue
            for part in range(2):
                if parts_lent[part][1] and k == parts_lent[part][0]:
                    lend(part, end).wait_recv()
            total = None
            for n in range(line - 1):
                if k == lent - 1:
                    lend_last(n, end).wait_recv()
                term = multiply(guest[:, k, :, n * depth:(n + 1) * depth], held[n + skipped, first_lent + k])
                total = term if total is None else total + term
            parts.append(total)
        return combine(jnp.concatenate(parts, axis=1))

    def split_rows(tile, at, target):
        for d in range(across):
            target[d, at * owned:(at + 1) * owned, :] = tile[d * owned:(d + 1) * owned]

    def visit(t):
        step, g = 1 + t // groups, t % groups
        from_left, from_right = me - step, me + step
        due_left, due_right = from_left >= 0, from_right < line
        if lent:
            wanted = jnp.logical_not(is_end) | (g < gone) | (g == groups - 1)
            due_left, due_right = due_left & wanted, due_right & wanted
        if extra:
            part = is_end & (g == mixed)
            due_left, due_right = due_left & jnp.logical_not(part), due_right & jnp.logical_not(part)

            @pl.when(part)
            def _():
                block = jnp.where(is_first, from_right, from_left)

                @pl.when((step > 1) | (cols == 0))
                def _():
                    hand_part(jnp.where(is_first, 1, 0), 0, block, beside_end).wait_recv()
                    acc[mixed] = acc[mixed] + of_block(block, mixed, per - extra)

                if cols:
                    @pl.when(step == 1)
                    def _():
                        hand_rest(jnp.where(is_first, 1, 0), block, beside_end).wait_recv()
                        columns = pl.ds(pl.multiple_of(block * depth + cols, LANES), depth - cols)
                        tile = multiply(resp[:, mixed * per, :, columns], held[block, mixed * per, :, cols:])
                        acc[mixed, :, :2 * focal] = acc[mixed, :, :2 * focal] + tile

        left_block, right_block = jnp.maximum(from_left, 0), jnp.minimum(from_right, line - 1)

        @pl.when(due_left)
        def _():
            hand_on(0, 0, left_block, g, left).wait_recv()

            @pl.when(has_right & (step < line - 1))
            def _():
                pass_on(0, step, left_block, g, right, lambda copy: copy.start())

        @pl.when(due_right)
        def _():
            hand_on(1, 0, right_block, g, right).wait_recv()

            @pl.when(has_left & (step < line - 1))
            def _():
                pass_on(1, step, right_block, g, left, lambda copy: copy.start())

        @pl.loop(0, 2)
        def _(side):
            @pl.when(((side == 0) & due_left) | ((side == 1) & due_right))
            def _():
                acc[g] = acc[g] + of_block(jnp.where(side == 0, left_block, right_block), g)

        if slots > 1:
            @pl.when(is_host & (step == line - 2) & (g == groups - 2))
            def _():
                for slot in range(slots - 1):
                    split_rows(serve(slot), slot, back_out)

    def visit_end():
        @pl.when(is_end)
        def _():
            block = jnp.where(is_first, line - 1, 0)
            columns = pl.ds(pl.multiple_of(block * depth, LANES), depth)
            parts = []
            for n in range(per):
                hand_last(jnp.where(is_first, 1, 0), block, n, beside_end).wait_recv()
                k = (groups - 1) * per + n
                parts.append(multiply(resp[:, k, :, columns], held[block, k]))
            acc[groups - 1] = acc[groups - 1] + jnp.concatenate(parts, axis=1)

    @pl.loop(0, (line - 1) * groups - 1)
    def _(t):
        visit(t)

    def partners():
        hops = list(range(1, across))
        if across & (across - 1):
            return [lax.rem(mine + hop, across) for hop in hops]
        hops.sort(key=lambda hop: -bin(hop >> 1).count("1"))
        bits = [1 << n for n in range(across.bit_length() - 1)]
        return [mine + sum(b * (1 - 2 * (mine // b % 2)) for b in bits if hop & b) for hop in hops]

    def exchange(part, source, target):
        for other in partners():
            pltpu.make_async_remote_copy(
                src_ref=source.at[other], dst_ref=target.at[mine],
                send_sem=x_send.at[part], recv_sem=x_recv.at[part],
                device_id={"freq": other}, device_id_type=MESH,
            ).start()
        target[mine] = source[mine]

    def exchanged(part, source, target):
        pltpu.make_async_remote_copy(
            src_ref=source.at[pl.ds(0, across - 1)], dst_ref=target.at[pl.ds(0, across - 1)],
            send_sem=x_send.at[part], recv_sem=x_recv.at[part],
            device_id={"freq": lax.rem(mine + 1, across)}, device_id_type=MESH,
        ).wait()

    def lines(source, r, g):
        return source[:, g * owned + r, :]

    def transform(pieces, place):
        parts = []
        for source, count in pieces:
            for g in range(count):
                rows_of = [lines(source, r, g) for r in range(owned)]
                for m in range(2 * per):
                    lanes = [row[:, m * focal:(m + 1) * focal] for row in rows_of]
                    parts.append(jnp.concatenate(lanes, axis=1))
        values = jnp.concatenate(parts, axis=0)
        high = values.astype(jnp.bfloat16)
        low = (values - high.astype(jnp.float32)).astype(jnp.bfloat16)
        first = place * 2 * per * across
        span = slice(first, first + values.shape[0])
        count = values.shape[1]

        def dot(a, b):
            return lax.dot_general(a, b, (((0,), (0,)), ((), ())), preferred_element_type=jnp.float32)

        return dot(high, table[0, span]) + (dot(low, table[0, span]) + dot(high, table[1, span]))

    for g in range(groups - 1):
        split_rows(combine(acc[g]), g, early_out)
    exchange(0, early_out, early_in)
    if slots:
        @pl.when(jnp.logical_not(is_end))
        def _():
            back_in[...] = jnp.zeros_like(back_in)

    load_table.wait()
    load_onset.wait()
    load_finale.wait()
    exchanged(0, early_out, early_in)
    traces[...] = transform([(early_in, groups - 1)], 0)
    visit_end()

    split_rows(combine(acc[groups - 1]), 0, late_out)
    exchange(1, late_out, late_in)

    if slots:
        @pl.when(is_host)
        def _():
            split_rows(serve(slots - 1), slots - 1, back_out)
            for other in partners() + [mine]:
                give_back(other, end).start()

    def drained(way, step, target):
        to_end = (me == line - 2) if way == 0 else (me == 1)

        def pieces(count):
            piece = held.at[me, pl.ds(0, count)]
            return pltpu.make_async_remote_copy(
                src_ref=piece, dst_ref=piece, send_sem=send_sem.at[way, step], recv_sem=recv_sem.at[0, 0],
                device_id={"recv": target}, device_id_type=MESH,
            )

        @pl.when(jnp.logical_not(to_end))
        def _():
            pieces(freqs).wait_send()

        @pl.when(to_end)
        def _():
            count = mixed * per if step == line - 2 else (mixed + 1) * per
            if count:
                pieces(count).wait_send()
            if extra and (step or not cols):
                hand_part(way, step, me, target).wait_send()
            if extra and cols and step == 0:
                hand_rest(way, me, target).wait_send()
            if step == line - 2:
                piece = held.at[me, pl.ds(0, per)]
                pltpu.make_async_remote_copy(
                    src_ref=piece, dst_ref=piece, send_sem=fine_send, recv_sem=fine_recv.at[0],
                    device_id={"recv": target}, device_id_type=MESH,
                ).wait_send()

    for step in range(line - 1):
        @pl.when(has_right & (me - step >= 0))
        def _():
            drained(0, step, right)

        @pl.when(has_left & (me + step < line))
        def _():
            drained(1, step, left)

    if slots:
        @pl.when(is_end)
        def _():
            pltpu.make_async_remote_copy(
                src_ref=guest, dst_ref=guest, send_sem=guest_send, recv_sem=guest_recv.at[0],
                device_id={"recv": beside_end}, device_id_type=MESH,
            ).wait_send()
            if cols:
                lend_morsel(beside_end, beside_end).wait_send()

        @pl.when(is_host)
        def _():
            all_back(end).wait_send()

    samples = lax.broadcasted_iota(jnp.int32, (focal, NT), 1)
    starts, ends = jnp.transpose(onset[...]), jnp.transpose(finale[...])
    exchanged(1, late_out, late_in)
    late_pieces = [(late_in, 1)]
    if slots:
        late_pieces = [(back_in, slots)] + late_pieces

        @pl.when(is_end)
        def _():
            all_back(beside_end).wait_recv()

    total = traces[...] + transform(late_pieces, groups - 1 - slots)
    for r in range(owned):
        inside = (samples >= starts[:, r:r + 1]) & (samples < ends[:, r:r + 1])
        windowed = jnp.where(inside, total[r * focal:(r + 1) * focal], 0.0)
        out_ref[:, r, :] = windowed


def per_device(line, across, response, focusing, window_onset, window_end):
    _, freqs, rows, sources = response.shape
    focal, depth = focusing.shape[2], focusing.shape[3]
    per = LANES // (2 * focal)
    groups = freqs // per
    owned = rows // across
    lent = lent_freqs(line, freqs, rows, focal, per)
    cols = lent_sources(line, freqs, rows, focal, per, lent, depth)
    slots = -(-lent // per)
    early_lines, late_lines, back_lines = (-(-count * owned // 8) * 8 for count in (groups - 1, 1, max(slots, 1)))
    tables = make_tables(across, groups, per)
    dma = pltpu.SemaphoreType.DMA
    return pl.pallas_call(
        functools.partial(spectra_kernel, line, across, lent, cols),
        out_shape=pltpu.VMEM((focal, owned, NT), jnp.float32),
        in_specs=[pl.BlockSpec(memory_space=pl.ANY)] * 5,
        out_specs=pl.BlockSpec(memory_space=pltpu.VMEM),
        scratch_shapes=[
            pltpu.VMEM(response.shape, jnp.bfloat16),
            pltpu.VMEM(focusing.shape, jnp.float32),
            pltpu.VMEM((line, freqs, 2 * focal, depth), jnp.bfloat16),
            pltpu.VMEM((2, max(lent, 1), rows, (line - 1) * depth), jnp.bfloat16),
            pltpu.VMEM((2, rows, max(cols, LANES)), jnp.bfloat16),
            pltpu.VMEM((groups, 2 * rows, LANES), jnp.float32),
            pltpu.VMEM((across, back_lines, LANES), jnp.float32),
            pltpu.VMEM((across, back_lines, LANES), jnp.float32),
            pltpu.VMEM(tables.shape, jnp.bfloat16),
            pltpu.VMEM((owned, focal), jnp.int32),
            pltpu.VMEM((owned, focal), jnp.int32),
            pltpu.VMEM((owned * focal, NT), jnp.float32),
            pltpu.VMEM((across, early_lines, LANES), jnp.float32),
            pltpu.VMEM((across, early_lines, LANES), jnp.float32),
            pltpu.VMEM((across, late_lines, LANES), jnp.float32),
            pltpu.VMEM((across, late_lines, LANES), jnp.float32),
            dma,
            dma((min(2, groups - 1) + 1,)),
            dma,
            dma,
            dma,
            dma((2, max(line - 1, 1))),
            dma((max(line - 1, 1),)),
            dma((max(line - 1, 1), groups)),
            dma,
            dma((per,)),
            dma,
            dma,
            dma((line + 2,)),
            dma,
            dma,
            dma((2,)),
            dma((2,)),
        ],
        compiler_params=pltpu.CompilerParams(
            collective_id=0, has_side_effects=True, vmem_limit_bytes=60000 * 1024
        ),
    )(response, focusing, tables, window_onset.T, window_end.T)


def solution(mesh):
    line, across = mesh.shape["recv"], mesh.shape["freq"]
    in_specs = (
        P(None, "freq", "recv", None),
        P(None, "freq", None, "recv"),
        P(None, ("recv", "freq")),
        P(None, ("recv", "freq")),
    )
    out_specs = P(None, ("recv", "freq"), None)
    return jax.shard_map(
        functools.partial(per_device, line, across),
        mesh=mesh, in_specs=in_specs, out_specs=out_specs, check_vma=False,
    )
```

```python
import functools
import math

import jax
import jax.numpy as jnp
import numpy as np
from jax import lax
from jax.experimental import pallas as pl
from jax.experimental.pallas import tpu as pltpu
from jax.sharding import PartitionSpec as P

NT = 1024
LANES = 128
MESH = pl.DeviceIdType.MESH


def make_tables(across, groups, per):
    freqs = groups * per
    count = across * freqs
    phase = (np.arange(count)[:, None] * np.arange(NT)[None, :] % NT) * (2.0 * math.pi / NT)
    scale = 1.0 / math.sqrt(count)
    table = np.stack([np.cos(phase) * scale, -np.sin(phase) * scale], 1)
    table = table.reshape(across, groups, per, 2, NT).transpose(1, 2, 3, 0, 4).reshape(-1, NT)
    high = table.astype(np.float32).astype(jnp.bfloat16)
    low = (table - high.astype(np.float64)).astype(np.float32).astype(jnp.bfloat16)
    return np.stack([high, low])


def lent_freqs(line, freqs, rows, focal, per):
    if line < 4:
        return 0
    even = (line - 2) * freqs * focal // ((line - 1) * (focal + rows))
    return max(min(even, freqs - per), 0)


def lent_sources(line, freqs, rows, focal, per, lent, depth):
    if lent % per != per - 1:
        return 0
    even = (line - 2) * freqs * focal * depth // (focal + rows) - (line - 1) * lent * depth
    return min(even // LANES * LANES, depth - LANES)


def spectra_kernel(
    line, across, lent, cols, resp_hbm, focus_hbm, table_hbm, onset_hbm, end_hbm, out_ref,
    resp, focus, held, guest, morsel, acc, back_out, back_in, table, onset, finale, traces,
    early_out, early_in, late_out, late_in,
    resp_sem, focus_sem, table_sem, onset_sem, finale_sem, send_sem, part_sem, recv_sem, fine_send, fine_recv,
    guest_send, morsel_send, guest_recv, back_send, back_recv, x_send, x_recv,
):
    me = lax.axis_index("recv")
    mine = lax.axis_index("freq")
    _, freqs, rows, _ = resp_hbm.shape
    focal, depth = focus_hbm.shape[2], focus_hbm.shape[3]
    groups = acc.shape[0]
    per = freqs // groups
    owned = rows // across
    slots = -(-lent // per)
    mixed = groups - 1 - slots
    extra = lent % per
    gone = mixed + 1 if extra else mixed
    first_lent = (groups - 1) * per - lent
    rear = max(min(lent, per) - 1, 0)
    parts_lent = [(0, max(lent - 1 - rear, 0)), (max(lent - 1 - rear, 0), rear)]
    has_left, has_right = me > 0, me < line - 1
    is_first, is_last = me == 0, me == line - 1
    left, right = jnp.maximum(me - 1, 0), jnp.minimum(me + 1, line - 1)
    is_end = is_first | is_last
    is_host = (me == 1) | (me == line - 2)
    beside_end = jnp.where(is_first, right, left)
    end = jnp.where(me == 1, 0, line - 1)
    skipped = jnp.where(is_first | (me == 1), 1, 0)

    leads = min(2, groups - 1)

    def load_focus(g):
        count = per if g < leads else (groups - leads) * per
        return pltpu.make_async_copy(
            focus_hbm.at[:, pl.ds(g * per, count)], focus.at[:, pl.ds(g * per, count)], focus_sem.at[g]
        )

    load_resp = pltpu.make_async_copy(resp_hbm, resp, resp_sem)

    for g in range(leads + 1):
        load_focus(g).start()

    barrier = pltpu.get_barrier_semaphore()

    @pl.when(has_left)
    def _():
        pl.semaphore_signal(barrier, inc=1, device_id={"recv": left}, device_id_type=MESH)

    @pl.when(has_right)
    def _():
        pl.semaphore_signal(barrier, inc=1, device_id={"recv": right}, device_id_type=MESH)

    for hop in range(1, across):
        other = lax.rem(mine + hop, across)
        pl.semaphore_signal(barrier, inc=1, device_id={"freq": other}, device_id_type=MESH)

    load_resp.start()

    load_table = pltpu.make_async_copy(table_hbm, table, table_sem)
    load_table.start()
    load_onset = pltpu.make_async_copy(onset_hbm, onset, onset_sem)
    load_onset.start()
    load_finale = pltpu.make_async_copy(end_hbm, finale, finale_sem)
    load_finale.start()

    def convert(g):
        for i in range(per):
            k = g * per + i
            for part in range(2):
                held[me, k, part * focal:(part + 1) * focal, :] = focus[part, k].astype(jnp.bfloat16)

    for g in range(leads):
        load_focus(g).wait()
        convert(g)

    beside = has_left.astype(jnp.int32) + has_right.astype(jnp.int32)
    pl.semaphore_wait(barrier, across - 1 + beside)

    def hand_on(way, step, block, g, target):
        piece = held.at[block, pl.ds(g * per, per)]
        return pltpu.make_async_remote_copy(
            src_ref=piece, dst_ref=piece,
            send_sem=send_sem.at[way, step], recv_sem=recv_sem.at[block - way, g],
            device_id={"recv": target}, device_id_type=MESH,
        )

    def hand_part(way, step, block, target):
        piece = held.at[block, pl.ds(mixed * per, per - extra)]
        return pltpu.make_async_remote_copy(
            src_ref=piece, dst_ref=piece,
            send_sem=part_sem.at[step], recv_sem=recv_sem.at[block - way, mixed],
            device_id={"recv": target}, device_id_type=MESH,
        )

    def hand_rest(way, block, target):
        piece = held.at[block, mixed * per, :, pl.ds(cols, depth - cols)]
        return pltpu.make_async_remote_copy(
            src_ref=piece, dst_ref=piece,
            send_sem=part_sem.at[0], recv_sem=recv_sem.at[block - way, mixed],
            device_id={"recv": target}, device_id_type=MESH,
        )

    def hand_last(way, block, n, target):
        piece = held.at[block, pl.ds((groups - 1) * per + n, 1)]
        return pltpu.make_async_remote_copy(
            src_ref=piece, dst_ref=piece,
            send_sem=fine_send, recv_sem=fine_recv.at[n],
            device_id={"recv": target}, device_id_type=MESH,
        )

    def pass_on(way, step, block, g, target, act):
        to_end = (me == line - 2) if way == 0 else (me == 1)
        last = to_end & (step == line - 2) & (g == groups - 1)
        part = to_end & (g == mixed) if extra else False
        plain = jnp.logical_not(last | part | (to_end & (g >= gone) & (g < groups - 1)))

        @pl.when(plain)
        def _():
            act(hand_on(way, step, block, g, target))

        @pl.when(last)
        def _():
            for n in range(per):
                act(hand_last(way, block, n, target))

        if extra:
            @pl.when(part & ((step > 0) | (cols == 0)))
            def _():
                act(hand_part(way, step, block, target))

            if cols:
                @pl.when(part & (step == 0))
                def _():
                    act(hand_rest(way, block, target))

    def lend(part, target):
        first, count = parts_lent[part]
        columns = pl.ds(pl.multiple_of(skipped * depth, LANES), (line - 1) * depth)
        return pltpu.make_async_remote_copy(
            src_ref=resp.at[:, pl.ds(first_lent + first, count), :, columns],
            dst_ref=guest.at[:, pl.ds(first, count)],
            send_sem=guest_send, recv_sem=guest_recv.at[part],
            device_id={"recv": target}, device_id_type=MESH,
        )

    def lend_morsel(host, target):
        columns = pl.ds(pl.multiple_of(host * depth, LANES), cols)
        return pltpu.make_async_remote_copy(
            src_ref=resp.at[:, mixed * per, :, columns], dst_ref=morsel,
            send_sem=morsel_send, recv_sem=guest_recv.at[2],
            device_id={"recv": target}, device_id_type=MESH,
        )

    def lend_last(n, target):
        columns = pl.ds(pl.multiple_of((n + skipped) * depth, LANES), depth)
        return pltpu.make_async_remote_copy(
            src_ref=resp.at[:, (groups - 1) * per - 1, :, columns],
            dst_ref=guest.at[:, lent - 1, :, pl.ds(n * depth, depth)],
            send_sem=guest_send, recv_sem=guest_recv.at[3 + n],
            device_id={"recv": target}, device_id_type=MESH,
        )

    def give_back(other, place):
        return pltpu.make_async_remote_copy(
            src_ref=back_out.at[other], dst_ref=back_in.at[mine], send_sem=back_send, recv_sem=back_recv,
            device_id={"recv": place, "freq": other}, device_id_type=MESH,
        )

    def all_back(place):
        return pltpu.make_async_remote_copy(
            src_ref=back_out, dst_ref=back_in, send_sem=back_send, recv_sem=back_recv,
            device_id={"recv": place}, device_id_type=MESH,
        )

    load_focus(leads).wait()

    @pl.loop(0, groups)
    def _(g):
        @pl.when(has_right)
        def _():
            pass_on(0, 0, me, g, right, lambda copy: copy.start())

        @pl.when(has_left)
        def _():
            pass_on(1, 0, me, g, left, lambda copy: copy.start())

        @pl.when(g + leads < groups)
        def _():
            convert(g + leads)

    def multiply(lhs, rhs):
        return lax.dot_general(
            lhs.reshape(2 * rows, lhs.shape[-1]), rhs, (((1,), (1,)), ((), ())),
            preferred_element_type=jnp.float32,
        )

    def of_block(block, g, count=per):
        columns = pl.ds(pl.multiple_of(block * depth, LANES), depth)
        parts = []
        for k in range(count):
            parts.append(multiply(resp[:, g * per + k, :, columns], held[block, g * per + k]))
        parts += [jnp.zeros((2 * rows, 2 * focal), jnp.float32)] * (per - count)
        return jnp.concatenate(parts, axis=1)

    load_resp.wait()

    if lent:
        @pl.when(is_end)
        def _():
            if cols:
                lend_morsel(beside_end, beside_end).start()
            for part in range(2):
                if parts_lent[part][1]:
                    lend(part, beside_end).start()
            for n in range(line - 1):
                lend_last(n, beside_end).start()

    @pl.loop(0, groups)
    def _(g):
        acc[g] = of_block(me, g)

    half = lax.rem(lax.broadcasted_iota(jnp.int32, (rows, LANES), 1), 2 * focal) < focal

    def combine(tile):
        real, imag = tile[:rows], tile[rows:]
        return real + jnp.where(
            half, -pltpu.roll(imag, LANES - focal, axis=1), pltpu.roll(imag, focal, axis=1)
        )

    def serve(slot):
        parts = []
        for n in range(per):
            k = lent - (slots - slot) * per + n
            if k == -1 and cols:
                lend_morsel(me, end).wait_recv()
                parts.append(multiply(morsel[...], held[me, mixed * per, :, :cols]))
                continue
            if k < 0:
                parts.append(jnp.zeros((2 * rows, 2 * focal), jnp.float32))
                continue
            for part in range(2):
                if parts_lent[part][1] and k == parts_lent[part][0]:
                    lend(part, end).wait_recv()
            total = None
            for n in range(line - 1):
                if k == lent - 1:
                    lend_last(n, end).wait_recv()
                term = multiply(guest[:, k, :, n * depth:(n + 1) * depth], held[n + skipped, first_lent + k])
                total = term if total is None else total + term
            parts.append(total)
        return combine(jnp.concatenate(parts, axis=1))

    def split_rows(tile, at, target):
        for d in range(across):
            target[d, at * owned:(at + 1) * owned, :] = tile[d * owned:(d + 1) * owned]

    def visit(t):
        step, g = 1 + t // groups, t % groups
        from_left, from_right = me - step, me + step
        due_left, due_right = from_left >= 0, from_right < line
        if lent:
            wanted = jnp.logical_not(is_end) | (g < gone) | (g == groups - 1)
            due_left, due_right = due_left & wanted, due_right & wanted
        if extra:
            part = is_end & (g == mixed)
            due_left, due_right = due_left & jnp.logical_not(part), due_right & jnp.logical_not(part)

            @pl.when(part)
            def _():
                block = jnp.where(is_first, from_right, from_left)

                @pl.when((step > 1) | (cols == 0))
                def _():
                    hand_part(jnp.where(is_first, 1, 0), 0, block, beside_end).wait_recv()
                    acc[mixed] = acc[mixed] + of_block(block, mixed, per - extra)

                if cols:
                    @pl.when(step == 1)
                    def _():
                        hand_rest(jnp.where(is_first, 1, 0), block, beside_end).wait_recv()
                        columns = pl.ds(pl.multiple_of(block * depth + cols, LANES), depth - cols)
                        tile = multiply(resp[:, mixed * per, :, columns], held[block, mixed * per, :, cols:])
                        acc[mixed, :, :2 * focal] = acc[mixed, :, :2 * focal] + tile

        left_block, right_block = jnp.maximum(from_left, 0), jnp.minimum(from_right, line - 1)

        @pl.when(due_left)
        def _():
            hand_on(0, 0, left_block, g, left).wait_recv()

            @pl.when(has_right & (step < line - 1))
            def _():
                pass_on(0, step, left_block, g, right, lambda copy: copy.start())

        @pl.when(due_right)
        def _():
            hand_on(1, 0, right_block, g, right).wait_recv()

            @pl.when(has_left & (step < line - 1))
            def _():
                pass_on(1, step, right_block, g, left, lambda copy: copy.start())

        @pl.loop(0, 2)
        def _(side):
            @pl.when(((side == 0) & due_left) | ((side == 1) & due_right))
            def _():
                acc[g] = acc[g] + of_block(jnp.where(side == 0, left_block, right_block), g)

        if slots > 1:
            @pl.when(is_host & (step == line - 2) & (g == groups - 2))
            def _():
                for slot in range(slots - 1):
                    split_rows(serve(slot), slot, back_out)

    def visit_end():
        @pl.when(is_end)
        def _():
            block = jnp.where(is_first, line - 1, 0)
            columns = pl.ds(pl.multiple_of(block * depth, LANES), depth)
            parts = []
            for n in range(per):
                hand_last(jnp.where(is_first, 1, 0), block, n, beside_end).wait_recv()
                k = (groups - 1) * per + n
                parts.append(multiply(resp[:, k, :, columns], held[block, k]))
            acc[groups - 1] = acc[groups - 1] + jnp.concatenate(parts, axis=1)

    @pl.loop(0, (line - 1) * groups - 1)
    def _(t):
        visit(t)

    def partners():
        hops = list(range(1, across))
        if across & (across - 1):
            return [lax.rem(mine + hop, across) for hop in hops]
        hops.sort(key=lambda hop: -bin(hop >> 1).count("1"))
        bits = [1 << n for n in range(across.bit_length() - 1)]
        return [mine + sum(b * (1 - 2 * (mine // b % 2)) for b in bits if hop & b) for hop in hops]

    def exchange(part, source, target):
        for other in partners():
            pltpu.make_async_remote_copy(
                src_ref=source.at[other], dst_ref=target.at[mine],
                send_sem=x_send.at[part], recv_sem=x_recv.at[part],
                device_id={"freq": other}, device_id_type=MESH,
            ).start()
        target[mine] = source[mine]

    def exchanged(part, source, target):
        pltpu.make_async_remote_copy(
            src_ref=source.at[pl.ds(0, across - 1)], dst_ref=target.at[pl.ds(0, across - 1)],
            send_sem=x_send.at[part], recv_sem=x_recv.at[part],
            device_id={"freq": lax.rem(mine + 1, across)}, device_id_type=MESH,
        ).wait()

    def lines(source, r, g):
        return source[:, g * owned + r, :]

    def transform(pieces, place):
        parts = []
        for source, count in pieces:
            for g in range(count):
                rows_of = [lines(source, r, g) for r in range(owned)]
                for m in range(2 * per):
                    lanes = [row[:, m * focal:(m + 1) * focal] for row in rows_of]
                    parts.append(jnp.concatenate(lanes, axis=1))
        values = jnp.concatenate(parts, axis=0)
        high = values.astype(jnp.bfloat16)
        low = (values - high.astype(jnp.float32)).astype(jnp.bfloat16)
        first = place * 2 * per * across
        span = slice(first, first + values.shape[0])
        count = values.shape[1]

        def dot(a, b):
            return lax.dot_general(a, b, (((0,), (0,)), ((), ())), preferred_element_type=jnp.float32)

        return dot(high, table[0, span]) + (dot(low, table[0, span]) + dot(high, table[1, span]))

    for g in range(groups - 1):
        split_rows(combine(acc[g]), g, early_out)
    exchange(0, early_out, early_in)
    load_table.wait()
    load_onset.wait()
    load_finale.wait()
    exchanged(0, early_out, early_in)
    traces[...] = transform([(early_in, groups - 1)], 0)
    visit_end()

    split_rows(combine(acc[groups - 1]), 0, late_out)
    exchange(1, late_out, late_in)

    if slots:
        @pl.when(is_host)
        def _():
            split_rows(serve(slots - 1), slots - 1, back_out)
            for other in partners() + [mine]:
                give_back(other, end).start()

    def drained(way, step, target):
        to_end = (me == line - 2) if way == 0 else (me == 1)

        def pieces(count):
            piece = held.at[me, pl.ds(0, count)]
            return pltpu.make_async_remote_copy(
                src_ref=piece, dst_ref=piece, send_sem=send_sem.at[way, step], recv_sem=recv_sem.at[0, 0],
                device_id={"recv": target}, device_id_type=MESH,
            )

        @pl.when(jnp.logical_not(to_end))
        def _():
            pieces(freqs).wait_send()

        @pl.when(to_end)
        def _():
            count = mixed * per if step == line - 2 else (mixed + 1) * per
            if count:
                pieces(count).wait_send()
            if extra and (step or not cols):
                hand_part(way, step, me, target).wait_send()
            if extra and cols and step == 0:
                hand_rest(way, me, target).wait_send()
            if step == line - 2:
                piece = held.at[me, pl.ds(0, per)]
                pltpu.make_async_remote_copy(
                    src_ref=piece, dst_ref=piece, send_sem=fine_send, recv_sem=fine_recv.at[0],
                    device_id={"recv": target}, device_id_type=MESH,
                ).wait_send()

    for step in range(line - 1):
        @pl.when(has_right & (me - step >= 0))
        def _():
            drained(0, step, right)

        @pl.when(has_left & (me + step < line))
        def _():
            drained(1, step, left)

    if slots:
        @pl.when(is_end)
        def _():
            pltpu.make_async_remote_copy(
                src_ref=guest, dst_ref=guest, send_sem=guest_send, recv_sem=guest_recv.at[0],
                device_id={"recv": beside_end}, device_id_type=MESH,
            ).wait_send()
            if cols:
                lend_morsel(beside_end, beside_end).wait_send()

        @pl.when(is_host)
        def _():
            all_back(end).wait_send()

    samples = lax.broadcasted_iota(jnp.int32, (focal, NT), 1)
    starts, ends = jnp.transpose(onset[...]), jnp.transpose(finale[...])
    if slots:
        @pl.when(is_end)
        def _():
            all_back(beside_end).wait_recv()
            traces[...] = traces[...] + transform([(back_in, slots)], groups - 1 - slots)

    insides = [(samples >= starts[:, r:r + 1]) & (samples < ends[:, r:r + 1]) for r in range(owned)]
    exchanged(1, late_out, late_in)
    total = traces[...] + transform([(late_in, 1)], groups - 1)
    for r in range(owned):
        windowed = jnp.where(insides[r], total[r * focal:(r + 1) * focal], 0.0)
        out_ref[:, r, :] = windowed


def per_device(line, across, response, focusing, window_onset, window_end):
    _, freqs, rows, sources = response.shape
    focal, depth = focusing.shape[2], focusing.shape[3]
    per = LANES // (2 * focal)
    groups = freqs // per
    owned = rows // across
    lent = lent_freqs(line, freqs, rows, focal, per)
    cols = lent_sources(line, freqs, rows, focal, per, lent, depth)
    slots = -(-lent // per)
    early_lines, late_lines, back_lines = (-(-count * owned // 8) * 8 for count in (groups - 1, 1, max(slots, 1)))
    tables = make_tables(across, groups, per)
    dma = pltpu.SemaphoreType.DMA
    return pl.pallas_call(
        functools.partial(spectra_kernel, line, across, lent, cols),
        out_shape=pltpu.VMEM((focal, owned, NT), jnp.float32),
        in_specs=[pl.BlockSpec(memory_space=pl.ANY)] * 5,
        out_specs=pl.BlockSpec(memory_space=pltpu.VMEM),
        scratch_shapes=[
            pltpu.VMEM(response.shape, jnp.bfloat16),
            pltpu.VMEM(focusing.shape, jnp.float32),
            pltpu.VMEM((line, freqs, 2 * focal, depth), jnp.bfloat16),
            pltpu.VMEM((2, max(lent, 1), rows, (line - 1) * depth), jnp.bfloat16),
            pltpu.VMEM((2, rows, max(cols, LANES)), jnp.bfloat16),
            pltpu.VMEM((groups, 2 * rows, LANES), jnp.float32),
            pltpu.VMEM((across, back_lines, LANES), jnp.float32),
            pltpu.VMEM((across, back_lines, LANES), jnp.float32),
            pltpu.VMEM(tables.shape, jnp.bfloat16),
            pltpu.VMEM((owned, focal), jnp.int32),
            pltpu.VMEM((owned, focal), jnp.int32),
            pltpu.VMEM((owned * focal, NT), jnp.float32),
            pltpu.VMEM((across, early_lines, LANES), jnp.float32),
            pltpu.VMEM((across, early_lines, LANES), jnp.float32),
            pltpu.VMEM((across, late_lines, LANES), jnp.float32),
            pltpu.VMEM((across, late_lines, LANES), jnp.float32),
            dma,
            dma((min(2, groups - 1) + 1,)),
            dma,
            dma,
            dma,
            dma((2, max(line - 1, 1))),
            dma((max(line - 1, 1),)),
            dma((max(line - 1, 1), groups)),
            dma,
            dma((per,)),
            dma,
            dma,
            dma((line + 2,)),
            dma,
            dma,
            dma((2,)),
            dma((2,)),
        ],
        compiler_params=pltpu.CompilerParams(
            collective_id=0, has_side_effects=True, vmem_limit_bytes=60000 * 1024
        ),
    )(response, focusing, tables, window_onset.T, window_end.T)


def solution(mesh):
    line, across = mesh.shape["recv"], mesh.shape["freq"]
    in_specs = (
        P(None, "freq", "recv", None),
        P(None, "freq", None, "recv"),
        P(None, ("recv", "freq")),
        P(None, ("recv", "freq")),
    )
    out_specs = P(None, ("recv", "freq"), None)
    return jax.shard_map(
        functools.partial(per_device, line, across),
        mesh=mesh, in_specs=in_specs, out_specs=out_specs, check_vma=False,
    )
```

```python
import functools
import math

import jax
import jax.numpy as jnp
import numpy as np
from jax import lax
from jax.experimental import pallas as pl
from jax.experimental.pallas import tpu as pltpu
from jax.sharding import PartitionSpec as P

NT = 1024
LANES = 128
MESH = pl.DeviceIdType.MESH


def make_tables(across, groups, per):
    freqs = groups * per
    count = across * freqs
    phase = (np.arange(count)[:, None] * np.arange(NT)[None, :] % NT) * (2.0 * math.pi / NT)
    scale = 1.0 / math.sqrt(count)
    table = np.stack([np.cos(phase) * scale, -np.sin(phase) * scale], 1)
    table = table.reshape(across, groups, per, 2, NT).transpose(1, 2, 3, 0, 4).reshape(-1, NT)
    high = table.astype(np.float32).astype(jnp.bfloat16)
    low = (table - high.astype(np.float64)).astype(np.float32).astype(jnp.bfloat16)
    return np.stack([high, low])


def lent_freqs(line, freqs, rows, focal, per):
    if line < 4:
        return 0
    even = (line - 2) * freqs * focal // ((line - 1) * (focal + rows))
    return max(min(even, freqs - per), 0)


def lent_sources(line, freqs, rows, focal, per, lent, depth):
    if lent % per != per - 1:
        return 0
    even = (line - 2) * freqs * focal * depth // (focal + rows) - (line - 1) * lent * depth
    return min(even // LANES * LANES, depth - LANES)


def spectra_kernel(
    line, across, lent, cols, resp_hbm, focus_hbm, table_hbm, onset_hbm, end_hbm, out_ref,
    resp, focus, held, guest, morsel, acc, back_out, back_in, table, onset, finale, traces,
    early_out, early_in, late_out, late_in,
    resp_sem, focus_sem, table_sem, onset_sem, finale_sem, send_sem, part_sem, recv_sem, fine_send, fine_recv,
    guest_send, morsel_send, guest_recv, back_send, back_recv, x_send, x_recv,
):
    me = lax.axis_index("recv")
    mine = lax.axis_index("freq")
    _, freqs, rows, _ = resp_hbm.shape
    focal, depth = focus_hbm.shape[2], focus_hbm.shape[3]
    groups = acc.shape[0]
    per = freqs // groups
    owned = rows // across
    slots = -(-lent // per)
    mixed = groups - 1 - slots
    extra = lent % per
    gone = mixed + 1 if extra else mixed
    first_lent = (groups - 1) * per - lent
    rear = max(min(lent, per) - 1, 0)
    parts_lent = [(0, max(lent - 1 - rear, 0)), (max(lent - 1 - rear, 0), rear)]
    has_left, has_right = me > 0, me < line - 1
    is_first, is_last = me == 0, me == line - 1
    left, right = jnp.maximum(me - 1, 0), jnp.minimum(me + 1, line - 1)
    is_end = is_first | is_last
    is_host = (me == 1) | (me == line - 2)
    beside_end = jnp.where(is_first, right, left)
    end = jnp.where(me == 1, 0, line - 1)
    skipped = jnp.where(is_first | (me == 1), 1, 0)

    leads = min(2, groups - 1)

    def load_focus(g):
        count = per if g < leads else (groups - leads) * per
        return pltpu.make_async_copy(
            focus_hbm.at[:, pl.ds(g * per, count)], focus.at[:, pl.ds(g * per, count)], focus_sem.at[g]
        )

    load_resp = pltpu.make_async_copy(resp_hbm, resp, resp_sem)

    for g in range(leads + 1):
        load_focus(g).start()

    barrier = pltpu.get_barrier_semaphore()

    @pl.when(has_left)
    def _():
        pl.semaphore_signal(barrier, inc=1, device_id={"recv": left}, device_id_type=MESH)

    @pl.when(has_right)
    def _():
        pl.semaphore_signal(barrier, inc=1, device_id={"recv": right}, device_id_type=MESH)

    for hop in range(1, across):
        other = lax.rem(mine + hop, across)
        pl.semaphore_signal(barrier, inc=1, device_id={"freq": other}, device_id_type=MESH)

    load_resp.start()

    load_table = pltpu.make_async_copy(table_hbm, table, table_sem)
    load_table.start()
    load_onset = pltpu.make_async_copy(onset_hbm, onset, onset_sem)
    load_onset.start()
    load_finale = pltpu.make_async_copy(end_hbm, finale, finale_sem)
    load_finale.start()

    def convert(g):
        for i in range(per):
            k = g * per + i
            for part in range(2):
                held[me, k, part * focal:(part + 1) * focal, :] = focus[part, k].astype(jnp.bfloat16)

    for g in range(leads):
        load_focus(g).wait()
        convert(g)

    beside = has_left.astype(jnp.int32) + has_right.astype(jnp.int32)
    pl.semaphore_wait(barrier, across - 1 + beside)

    def hand_on(way, step, block, g, target):
        piece = held.at[block, pl.ds(g * per, per)]
        return pltpu.make_async_remote_copy(
            src_ref=piece, dst_ref=piece,
            send_sem=send_sem.at[way, step], recv_sem=recv_sem.at[block - way, g],
            device_id={"recv": target}, device_id_type=MESH,
        )

    def hand_part(way, step, block, target):
        piece = held.at[block, pl.ds(mixed * per, per - extra)]
        return pltpu.make_async_remote_copy(
            src_ref=piece, dst_ref=piece,
            send_sem=part_sem.at[step], recv_sem=recv_sem.at[block - way, mixed],
            device_id={"recv": target}, device_id_type=MESH,
        )

    def hand_rest(way, block, target):
        piece = held.at[block, mixed * per, :, pl.ds(cols, depth - cols)]
        return pltpu.make_async_remote_copy(
            src_ref=piece, dst_ref=piece,
            send_sem=part_sem.at[0], recv_sem=recv_sem.at[block - way, mixed],
            device_id={"recv": target}, device_id_type=MESH,
        )

    def hand_last(way, block, n, target):
        k, columns = (groups - 1) * per + min(n, per - 1), pl.ds(0, depth)
        if n >= per - 1:
            columns = pl.ds((n - per + 1) * (depth // 2), depth // 2)
        piece = held.at[block, pl.ds(k, 1), :, columns]
        return pltpu.make_async_remote_copy(
            src_ref=piece, dst_ref=piece,
            send_sem=fine_send, recv_sem=fine_recv.at[n],
            device_id={"recv": target}, device_id_type=MESH,
        )

    def pass_on(way, step, block, g, target, act):
        to_end = (me == line - 2) if way == 0 else (me == 1)
        last = to_end & (step == line - 2) & (g == groups - 1)
        part = to_end & (g == mixed) if extra else False
        plain = jnp.logical_not(last | part | (to_end & (g >= gone) & (g < groups - 1)))

        @pl.when(plain)
        def _():
            act(hand_on(way, step, block, g, target))

        @pl.when(last)
        def _():
            for n in range(per + 1):
                act(hand_last(way, block, n, target))

        if extra:
            @pl.when(part & ((step > 0) | (cols == 0)))
            def _():
                act(hand_part(way, step, block, target))

            if cols:
                @pl.when(part & (step == 0))
                def _():
                    act(hand_rest(way, block, target))

    def lend(part, target):
        first, count = parts_lent[part]
        columns = pl.ds(pl.multiple_of(skipped * depth, LANES), (line - 1) * depth)
        return pltpu.make_async_remote_copy(
            src_ref=resp.at[:, pl.ds(first_lent + first, count), :, columns],
            dst_ref=guest.at[:, pl.ds(first, count)],
            send_sem=guest_send, recv_sem=guest_recv.at[part],
            device_id={"recv": target}, device_id_type=MESH,
        )

    def lend_morsel(host, target):
        columns = pl.ds(pl.multiple_of(host * depth, LANES), cols)
        return pltpu.make_async_remote_copy(
            src_ref=resp.at[:, mixed * per, :, columns], dst_ref=morsel,
            send_sem=morsel_send, recv_sem=guest_recv.at[2],
            device_id={"recv": target}, device_id_type=MESH,
        )

    def lend_last(n, target):
        columns = pl.ds(pl.multiple_of((n + skipped) * depth, LANES), depth)
        return pltpu.make_async_remote_copy(
            src_ref=resp.at[:, (groups - 1) * per - 1, :, columns],
            dst_ref=guest.at[:, lent - 1, :, pl.ds(n * depth, depth)],
            send_sem=guest_send, recv_sem=guest_recv.at[3 + n],
            device_id={"recv": target}, device_id_type=MESH,
        )

    def give_back(other, place):
        return pltpu.make_async_remote_copy(
            src_ref=back_out.at[other], dst_ref=back_in.at[mine], send_sem=back_send, recv_sem=back_recv,
            device_id={"recv": place, "freq": other}, device_id_type=MESH,
        )

    def all_back(place):
        return pltpu.make_async_remote_copy(
            src_ref=back_out, dst_ref=back_in, send_sem=back_send, recv_sem=back_recv,
            device_id={"recv": place}, device_id_type=MESH,
        )

    load_focus(leads).wait()

    @pl.loop(0, groups)
    def _(g):
        @pl.when(has_right)
        def _():
            pass_on(0, 0, me, g, right, lambda copy: copy.start())

        @pl.when(has_left)
        def _():
            pass_on(1, 0, me, g, left, lambda copy: copy.start())

        @pl.when(g + leads < groups)
        def _():
            convert(g + leads)

    def multiply(lhs, rhs):
        return lax.dot_general(
            lhs.reshape(2 * rows, lhs.shape[-1]), rhs, (((1,), (1,)), ((), ())),
            preferred_element_type=jnp.float32,
        )

    def of_block(block, g, count=per):
        columns = pl.ds(pl.multiple_of(block * depth, LANES), depth)
        parts = []
        for k in range(count):
            parts.append(multiply(resp[:, g * per + k, :, columns], held[block, g * per + k]))
        parts += [jnp.zeros((2 * rows, 2 * focal), jnp.float32)] * (per - count)
        return jnp.concatenate(parts, axis=1)

    load_resp.wait()

    if lent:
        @pl.when(is_end)
        def _():
            if cols:
                lend_morsel(beside_end, beside_end).start()
            for part in range(2):
                if parts_lent[part][1]:
                    lend(part, beside_end).start()
            for n in range(line - 1):
                lend_last(n, beside_end).start()

    @pl.loop(0, groups)
    def _(g):
        acc[g] = of_block(me, g)

    half = lax.rem(lax.broadcasted_iota(jnp.int32, (rows, LANES), 1), 2 * focal) < focal

    def combine(tile):
        real, imag = tile[:rows], tile[rows:]
        return real + jnp.where(
            half, -pltpu.roll(imag, LANES - focal, axis=1), pltpu.roll(imag, focal, axis=1)
        )

    def serve(slot):
        parts = []
        for n in range(per):
            k = lent - (slots - slot) * per + n
            if k == -1 and cols:
                lend_morsel(me, end).wait_recv()
                parts.append(multiply(morsel[...], held[me, mixed * per, :, :cols]))
                continue
            if k < 0:
                parts.append(jnp.zeros((2 * rows, 2 * focal), jnp.float32))
                continue
            for part in range(2):
                if parts_lent[part][1] and k == parts_lent[part][0]:
                    lend(part, end).wait_recv()
            total = None
            for n in range(line - 1):
                if k == lent - 1:
                    lend_last(n, end).wait_recv()
                term = multiply(guest[:, k, :, n * depth:(n + 1) * depth], held[n + skipped, first_lent + k])
                total = term if total is None else total + term
            parts.append(total)
        return combine(jnp.concatenate(parts, axis=1))

    def split_rows(tile, at, target):
        for d in range(across):
            target[d, at * owned:(at + 1) * owned, :] = tile[d * owned:(d + 1) * owned]

    def visit(t):
        step, g = 1 + t // groups, t % groups
        from_left, from_right = me - step, me + step
        due_left, due_right = from_left >= 0, from_right < line
        if lent:
            wanted = jnp.logical_not(is_end) | (g < gone) | (g == groups - 1)
            due_left, due_right = due_left & wanted, due_right & wanted
        if extra:
            part = is_end & (g == mixed)
            due_left, due_right = due_left & jnp.logical_not(part), due_right & jnp.logical_not(part)

            @pl.when(part)
            def _():
                block = jnp.where(is_first, from_right, from_left)

                @pl.when((step > 1) | (cols == 0))
                def _():
                    hand_part(jnp.where(is_first, 1, 0), 0, block, beside_end).wait_recv()
                    acc[mixed] = acc[mixed] + of_block(block, mixed, per - extra)

                if cols:
                    @pl.when(step == 1)
                    def _():
                        hand_rest(jnp.where(is_first, 1, 0), block, beside_end).wait_recv()
                        columns = pl.ds(pl.multiple_of(block * depth + cols, LANES), depth - cols)
                        tile = multiply(resp[:, mixed * per, :, columns], held[block, mixed * per, :, cols:])
                        acc[mixed, :, :2 * focal] = acc[mixed, :, :2 * focal] + tile

        left_block, right_block = jnp.maximum(from_left, 0), jnp.minimum(from_right, line - 1)

        @pl.when(due_left)
        def _():
            hand_on(0, 0, left_block, g, left).wait_recv()

            @pl.when(has_right & (step < line - 1))
            def _():
                pass_on(0, step, left_block, g, right, lambda copy: copy.start())

        @pl.when(due_right)
        def _():
            hand_on(1, 0, right_block, g, right).wait_recv()

            @pl.when(has_left & (step < line - 1))
            def _():
                pass_on(1, step, right_block, g, left, lambda copy: copy.start())

        @pl.loop(0, 2)
        def _(side):
            @pl.when(((side == 0) & due_left) | ((side == 1) & due_right))
            def _():
                acc[g] = acc[g] + of_block(jnp.where(side == 0, left_block, right_block), g)

        if slots > 1:
            @pl.when(is_host & (step == line - 2) & (g == groups - 2))
            def _():
                for slot in range(slots - 1):
                    split_rows(serve(slot), slot, back_out)

    def visit_end():
        @pl.when(is_end)
        def _():
            block = jnp.where(is_first, line - 1, 0)
            columns = pl.ds(pl.multiple_of(block * depth, LANES), depth)
            parts = []
            for n in range(per):
                hand_last(jnp.where(is_first, 1, 0), block, n, beside_end).wait_recv()
                k = (groups - 1) * per + n
                if n < per - 1:
                    parts.append(multiply(resp[:, k, :, columns], held[block, k]))
                    continue
                near = pl.ds(pl.multiple_of(block * depth, LANES), depth // 2)
                far = pl.ds(pl.multiple_of(block * depth + depth // 2, LANES), depth // 2)
                tile = multiply(resp[:, k, :, near], held[block, k, :, :depth // 2])
                hand_last(jnp.where(is_first, 1, 0), block, per, beside_end).wait_recv()
                parts.append(tile + multiply(resp[:, k, :, far], held[block, k, :, depth // 2:]))
            acc[groups - 1] = acc[groups - 1] + jnp.concatenate(parts, axis=1)

    @pl.loop(0, (line - 1) * groups - 1)
    def _(t):
        visit(t)

    def partners():
        hops = list(range(1, across))
        if across & (across - 1):
            return [lax.rem(mine + hop, across) for hop in hops]
        hops.sort(key=lambda hop: -bin(hop >> 1).count("1"))
        bits = [1 << n for n in range(across.bit_length() - 1)]
        return [mine + sum(b * (1 - 2 * (mine // b % 2)) for b in bits if hop & b) for hop in hops]

    def exchange(part, source, target):
        for other in partners():
            pltpu.make_async_remote_copy(
                src_ref=source.at[other], dst_ref=target.at[mine],
                send_sem=x_send.at[part], recv_sem=x_recv.at[part],
                device_id={"freq": other}, device_id_type=MESH,
            ).start()
        target[mine] = source[mine]

    def exchanged(part, source, target):
        pltpu.make_async_remote_copy(
            src_ref=source.at[pl.ds(0, across - 1)], dst_ref=target.at[pl.ds(0, across - 1)],
            send_sem=x_send.at[part], recv_sem=x_recv.at[part],
            device_id={"freq": lax.rem(mine + 1, across)}, device_id_type=MESH,
        ).wait()

    def lines(source, r, g):
        return source[:, g * owned + r, :]

    def transform(pieces, place):
        parts = []
        for source, count in pieces:
            for g in range(count):
                rows_of = [lines(source, r, g) for r in range(owned)]
                for m in range(2 * per):
                    lanes = [row[:, m * focal:(m + 1) * focal] for row in rows_of]
                    parts.append(jnp.concatenate(lanes, axis=1))
        values = jnp.concatenate(parts, axis=0)
        high = values.astype(jnp.bfloat16)
        low = (values - high.astype(jnp.float32)).astype(jnp.bfloat16)
        first = place * 2 * per * across
        span = slice(first, first + values.shape[0])
        count = values.shape[1]

        def dot(a, b):
            return lax.dot_general(a, b, (((0,), (0,)), ((), ())), preferred_element_type=jnp.float32)

        return dot(high, table[0, span]) + (dot(low, table[0, span]) + dot(high, table[1, span]))

    for g in range(groups - 1):
        split_rows(combine(acc[g]), g, early_out)
    exchange(0, early_out, early_in)
    load_table.wait()
    load_onset.wait()
    load_finale.wait()
    exchanged(0, early_out, early_in)
    traces[...] = transform([(early_in, groups - 1)], 0)
    visit_end()

    split_rows(combine(acc[groups - 1]), 0, late_out)
    exchange(1, late_out, late_in)

    if slots:
        @pl.when(is_host)
        def _():
            split_rows(serve(slots - 1), slots - 1, back_out)
            for other in partners() + [mine]:
                give_back(other, end).start()

    def drained(way, step, target):
        to_end = (me == line - 2) if way == 0 else (me == 1)

        def pieces(count):
            piece = held.at[me, pl.ds(0, count)]
            return pltpu.make_async_remote_copy(
                src_ref=piece, dst_ref=piece, send_sem=send_sem.at[way, step], recv_sem=recv_sem.at[0, 0],
                device_id={"recv": target}, device_id_type=MESH,
            )

        @pl.when(jnp.logical_not(to_end))
        def _():
            pieces(freqs).wait_send()

        @pl.when(to_end)
        def _():
            count = mixed * per if step == line - 2 else (mixed + 1) * per
            if count:
                pieces(count).wait_send()
            if extra and (step or not cols):
                hand_part(way, step, me, target).wait_send()
            if extra and cols and step == 0:
                hand_rest(way, me, target).wait_send()
            if step == line - 2:
                piece = held.at[me, pl.ds(0, per)]
                pltpu.make_async_remote_copy(
                    src_ref=piece, dst_ref=piece, send_sem=fine_send, recv_sem=fine_recv.at[0],
                    device_id={"recv": target}, device_id_type=MESH,
                ).wait_send()

    for step in range(line - 1):
        @pl.when(has_right & (me - step >= 0))
        def _():
            drained(0, step, right)

        @pl.when(has_left & (me + step < line))
        def _():
            drained(1, step, left)

    if slots:
        @pl.when(is_end)
        def _():
            pltpu.make_async_remote_copy(
                src_ref=guest, dst_ref=guest, send_sem=guest_send, recv_sem=guest_recv.at[0],
                device_id={"recv": beside_end}, device_id_type=MESH,
            ).wait_send()
            if cols:
                lend_morsel(beside_end, beside_end).wait_send()

        @pl.when(is_host)
        def _():
            all_back(end).wait_send()

    samples = lax.broadcasted_iota(jnp.int32, (focal, NT), 1)
    starts, ends = jnp.transpose(onset[...]), jnp.transpose(finale[...])
    if slots:
        @pl.when(is_end)
        def _():
            all_back(beside_end).wait_recv()
            traces[...] = traces[...] + transform([(back_in, slots)], groups - 1 - slots)

    insides = [(samples >= starts[:, r:r + 1]) & (samples < ends[:, r:r + 1]) for r in range(owned)]
    exchanged(1, late_out, late_in)
    total = traces[...] + transform([(late_in, 1)], groups - 1)
    for r in range(owned):
        windowed = jnp.where(insides[r], total[r * focal:(r + 1) * focal], 0.0)
        out_ref[:, r, :] = windowed


def per_device(line, across, response, focusing, window_onset, window_end):
    _, freqs, rows, sources = response.shape
    focal, depth = focusing.shape[2], focusing.shape[3]
    per = LANES // (2 * focal)
    groups = freqs // per
    owned = rows // across
    lent = lent_freqs(line, freqs, rows, focal, per)
    cols = lent_sources(line, freqs, rows, focal, per, lent, depth)
    slots = -(-lent // per)
    early_lines, late_lines, back_lines = (-(-count * owned // 8) * 8 for count in (groups - 1, 1, max(slots, 1)))
    tables = make_tables(across, groups, per)
    dma = pltpu.SemaphoreType.DMA
    return pl.pallas_call(
        functools.partial(spectra_kernel, line, across, lent, cols),
        out_shape=pltpu.VMEM((focal, owned, NT), jnp.float32),
        in_specs=[pl.BlockSpec(memory_space=pl.ANY)] * 5,
        out_specs=pl.BlockSpec(memory_space=pltpu.VMEM),
        scratch_shapes=[
            pltpu.VMEM(response.shape, jnp.bfloat16),
            pltpu.VMEM(focusing.shape, jnp.float32),
            pltpu.VMEM((line, freqs, 2 * focal, depth), jnp.bfloat16),
            pltpu.VMEM((2, max(lent, 1), rows, (line - 1) * depth), jnp.bfloat16),
            pltpu.VMEM((2, rows, max(cols, LANES)), jnp.bfloat16),
            pltpu.VMEM((groups, 2 * rows, LANES), jnp.float32),
            pltpu.VMEM((across, back_lines, LANES), jnp.float32),
            pltpu.VMEM((across, back_lines, LANES), jnp.float32),
            pltpu.VMEM(tables.shape, jnp.bfloat16),
            pltpu.VMEM((owned, focal), jnp.int32),
            pltpu.VMEM((owned, focal), jnp.int32),
            pltpu.VMEM((owned * focal, NT), jnp.float32),
            pltpu.VMEM((across, early_lines, LANES), jnp.float32),
            pltpu.VMEM((across, early_lines, LANES), jnp.float32),
            pltpu.VMEM((across, late_lines, LANES), jnp.float32),
            pltpu.VMEM((across, late_lines, LANES), jnp.float32),
            dma,
            dma((min(2, groups - 1) + 1,)),
            dma,
            dma,
            dma,
            dma((2, max(line - 1, 1))),
            dma((max(line - 1, 1),)),
            dma((max(line - 1, 1), groups)),
            dma,
            dma((per + 1,)),
            dma,
            dma,
            dma((line + 2,)),
            dma,
            dma,
            dma((2,)),
            dma((2,)),
        ],
        compiler_params=pltpu.CompilerParams(
            collective_id=0, has_side_effects=True, vmem_limit_bytes=60000 * 1024
        ),
    )(response, focusing, tables, window_onset.T, window_end.T)


def solution(mesh):
    line, across = mesh.shape["recv"], mesh.shape["freq"]
    in_specs = (
        P(None, "freq", "recv", None),
        P(None, "freq", None, "recv"),
        P(None, ("recv", "freq")),
        P(None, ("recv", "freq")),
    )
    out_specs = P(None, ("recv", "freq"), None)
    return jax.shard_map(
        functools.partial(per_device, line, across),
        mesh=mesh, in_specs=in_specs, out_specs=out_specs, check_vma=False,
    )
```
